256 devices in a mesh: rep: 32 (over z_lo, x, core), shard: 8 (over y, z_hi).
Axes of the slice: x: 4, y: 4, z: 8 (z_hi: 2, z_lo: 4; z = z_hi * 4 + z_lo), core: 2. Of those that a mesh axis runs over, the one named last changes fastest.
Arguments:
- latents: bfloat16 [256, 32, 32, 640], P(('rep', 'shard'))
- cotangent: bfloat16 [256, 32, 32, 640], P(('rep', 'shard')), may hold values from -6 to 6
- gn_gain: float32 [640], replicated, may hold values from 0.1 to 1.9
- gn_bias: float32 [640], replicated, may hold values from -3 to 3
- conv_weight: bfloat16 [5760, 640], P('shard'), may hold values from -0.078125 to 0.078125
- master: float32 [640, 5760], P('rep', 'shard'), may hold values from -6 to 6
- moment_one: float32 [640, 5760], P('rep', 'shard'), may hold values from -6 to 6
- moment_two: float32 [640, 5760], P('rep', 'shard'), may hold values from 0.1 to 10
- departing: int32 [32], replicated, may hold values from 0 to 1, as said below
- partner: int32 [32], replicated, may hold values from 0 to 31, as said below
Outputs:
- conv_out: bfloat16 [256, 32, 32, 640], P(('rep', 'shard'))
- new_master: float32 [32, 2, 20, 5760], P('rep', None, None, 'shard')
- new_first: float32 [32, 2, 20, 5760], P('rep', None, None, 'shard')
- new_second: float32 [32, 2, 20, 5760], P('rep', None, None, 'shard')
The draws below stay inside these ranges and needn't reach their ends.
Inputs may be any that keep to these rules, and one draw needn't show every extreme that they name: Exactly 16 replicas have departing = 1. partner pairs each departing replica with one staying replica and back: partner[partner[r]] = r and departing[partner[r]] = 1 - departing[r]; at least one replica r has partner[r] = (r + 16) mod 32.
All inputs are finite; a program needn't handle non-finite values.
Results may differ from the reference program's by a relative error of at most 0.007.
Values may be sent and summed in bfloat16 or wider, within the bound.
A program may use at most 128 MiB of HBM per device.

```python
import math
import jax
import jax.numpy as jnp
from jax import lax

CIN = 640
COUT = 640
GROUPS = 32
H = 32
WID = 32
IMG_REP = 8
KIN = 5760
IMAGES = 256
N_REP = 32
N_SHARD = 8


def pairing(key):
    half_count = N_REP // 2
    first_fixed = jax.random.randint(jax.random.fold_in(key, 5), (), 0, N_REP).astype(jnp.int32)
    second_fixed = ((first_fixed + half_count) % N_REP).astype(jnp.int32)
    index_all = jnp.arange(N_REP, dtype=jnp.int32)
    ranks = jax.random.permutation(jax.random.fold_in(key, 7), N_REP).astype(jnp.int32)
    scores = jnp.where(index_all == first_fixed, N_REP, jnp.where(index_all == second_fixed, N_REP + 1, ranks)).astype(jnp.int32)
    order = jnp.argsort(scores, stable=True).astype(jnp.int32)
    first_side = jnp.concatenate([order[:half_count - 1], order[N_REP - 2:N_REP - 1]])
    second_side = jnp.concatenate([order[half_count - 1:N_REP - 2], order[N_REP - 1:]])
    flips = jax.random.randint(jax.random.fold_in(key, 9), (half_count,), 0, 2).astype(jnp.int32)
    leavers = jnp.where(flips == 1, first_side, second_side).astype(jnp.int32)
    stayers = jnp.where(flips == 1, second_side, first_side).astype(jnp.int32)
    leaving = jnp.zeros((N_REP,), jnp.int32).at[leavers].set(1)
    mates = jnp.zeros((N_REP,), jnp.int32).at[leavers].set(stayers)
    mates = mates.at[stayers].set(leavers)
    return (leaving, mates)


def draw_departing(key, part):
    return pairing(key)[0]


def draw_partner(key, part):
    return pairing(key)[1]


def draw_latents(key, part):
    key_a = jax.random.fold_in(key, 11)
    key_b = jax.random.fold_in(key, 12)
    row_scale = 1.0 + 2.0 * jnp.arange(H, dtype=jnp.float32) / (H - 1)
    chan_scale = jax.random.uniform(key_b, (CIN,), jnp.float32, 0.5, 2.0)
    values = jax.random.normal(key_a, (IMAGES, H, WID, CIN), jnp.float32) * row_scale[:, None, None] * chan_scale
    return values.astype(jnp.bfloat16)


def block_scale(rng, dims, cuts, low, top_value):
    def one(position, parts):
        draws = jax.random.uniform(jax.random.fold_in(jax.random.fold_in(rng, 6), position), (parts,), jnp.float32, low / len(cuts), top_value / len(cuts))
        return jnp.repeat(jnp.exp(draws), dims[position] // parts).reshape((-1,) + (1,) * (len(dims) - position - 1))

    factor_of = one(*cuts[0])
    for cut in cuts[1:]:
        factor_of = factor_of * one(*cut)
    return factor_of


def gaussian(rng, extent, scale, most, split=(), held_as=jnp.bfloat16):
    array = scale * jax.random.normal(rng, extent, jnp.float32)
    if split:
        array = array * block_scale(rng, extent, split, -0.22, 0.18)
    return jnp.clip(array, -most, most).astype(held_as)


def setup_inputs(seed: int = 0) -> dict:
    key_of = jax.random.split(jax.random.key(seed), 11)
    return {
        "latents": draw_latents(jax.random.fold_in(key_of[10], 71), 0),
        "cotangent": gaussian(key_of[1], (IMAGES, H, WID, COUT), 1.0, 6.0, ((0, 256),)),
        "gn_gain": jnp.clip(1.0 + 0.18 * jax.random.normal(key_of[2], (CIN,), jnp.float32), 0.1, 1.9),
        "gn_bias": gaussian(key_of[3], (CIN,), 0.5, 3.0, (), jnp.float32),
        "conv_weight": gaussian(key_of[4], (KIN, COUT), KIN ** -0.5, 0.078125, ((0, 8),)),
        "master": gaussian(key_of[5], (COUT, KIN), 1.0, 6.0, ((0, 32), (1, 8)), jnp.float32),
        "moment_one": gaussian(key_of[6], (COUT, KIN), 1.0, 6.0, ((0, 32), (1, 8)), jnp.float32),
        "moment_two": jnp.clip(jnp.exp(math.log(10.0) - 4.6051702 * jax.random.uniform(key_of[7], (COUT, KIN), jnp.float32) ** block_scale(key_of[7], (COUT, KIN), ((0, 32), (1, 8)), -0.2, 0.2)), 0.1, 10.0),
        "departing": draw_departing(jax.random.fold_in(key_of[10], 71), 0),
        "partner": draw_partner(jax.random.fold_in(key_of[10], 71), 0),
    }


beta_one = 0.9
beta_two = 0.999
step_count = 100.0
learn_rate = 0.01
weight_decay = 0.01
adam_eps = 1e-08
norm_eps = 1e-05

def activate(latent_rep, gn_gain, gn_bias):
    float_in = latent_rep.astype(jnp.float32)
    group_width = CIN // GROUPS
    pixel_count = H * WID * group_width
    chan_sums = lax.optimization_barrier(jnp.sum(float_in, axis=(1, 2)))
    group_mean = chan_sums.reshape(-1, GROUPS, group_width).sum(-1) / pixel_count
    centred = float_in - jnp.repeat(group_mean, group_width, axis=1)[:, None, None, :]
    squares = lax.optimization_barrier(jnp.sum(centred * centred, axis=(1, 2))).reshape(-1, GROUPS, group_width).sum(-1)
    variance = squares / pixel_count
    inverse = jnp.repeat(lax.rsqrt(variance + norm_eps), group_width, axis=1)[:, None, None, :]
    return jax.nn.silu(centred * inverse * gn_gain + gn_bias).astype(jnp.bfloat16)

def gather_taps(padded, row_count, col_count):
    taps = [padded[:, row_off:row_off + row_count, col_off:col_off + col_count, :] for row_off in range(3) for col_off in range(3)]
    return jnp.concatenate(taps, axis=3)

def adam(master, first_moment, second_moment, gradient):
    first_moment = beta_one * first_moment + (1.0 - beta_one) * gradient
    second_moment = beta_two * second_moment + (1.0 - beta_two) * gradient * gradient
    first_hat = first_moment / (1.0 - beta_one ** step_count)
    second_hat = second_moment / (1.0 - beta_two ** step_count)
    master = master - learn_rate * (first_hat / (jnp.sqrt(second_hat) + adam_eps) + weight_decay * master)
    return (master, first_moment, second_moment)

def reference(latents, cotangent, gn_gain, gn_bias, conv_weight, master, moment_one, moment_two, departing, partner):
    img_dev = IMG_REP // N_SHARD
    weight_f = conv_weight.astype(jnp.float32)
    latent_reps = latents.reshape(N_REP, IMG_REP, H, WID, CIN)
    cot_reps = cotangent.reshape(N_REP, IMG_REP, H, WID, COUT)
    staying = (1 - departing).astype(jnp.float32)

    def replica(summed, inputs):
        latent_rep, cot_rep, stay_rep = inputs
        activated = activate(latent_rep, gn_gain, gn_bias)
        padded = jnp.pad(activated, ((0, 0), (1, 1), (1, 1), (0, 0)))
        patches = gather_taps(padded, H, WID).astype(jnp.float32)
        conv_rep = jnp.einsum('ihwk,kc->ihwc', patches, weight_f).astype(jnp.bfloat16)
        blocks = patches.reshape(N_SHARD, img_dev * H * WID, 9 * CIN)
        cot_blocks = cot_rep.astype(jnp.float32).reshape(N_SHARD, img_dev * H * WID, COUT)
        partial_value = jnp.einsum('spk,spc->skc', blocks, cot_blocks).astype(jnp.bfloat16)
        partial_value = lax.optimization_barrier(partial_value).astype(jnp.float32)
        return (summed + stay_rep * lax.optimization_barrier(jnp.sum(partial_value, axis=0)), conv_rep)
    summed, conv_out = lax.scan(replica, jnp.zeros((9 * CIN, COUT), jnp.float32), (latent_reps, cot_reps, staying))
    gradient = (summed / (IMG_REP * (N_REP // 2))).T
    next_master, next_first, next_second = adam(master, moment_one, moment_two, gradient)
    block_cols = COUT // N_REP

    def arrange(state):
        blocks = state.reshape(N_REP, block_cols, 9 * CIN)
        paired = jnp.stack([blocks, blocks[partner]], axis=1)
        return paired * staying[:, None, None, None]
    return (conv_out.reshape(IMAGES, H, WID, COUT), arrange(next_master), arrange(next_first), arrange(next_second))
```

```python
import jax
import jax.numpy as jnp
from jax import lax
from jax.experimental import pallas as pl
from jax.experimental.pallas import tpu as pltpu
from jax.sharding import PartitionSpec as P

GROUPS = 32
MESH = pl.DeviceIdType.MESH
F32 = jnp.float32
BF16 = jnp.bfloat16

beta_one = 0.9
beta_two = 0.999
step_count = 100.0
learn_rate = 0.01
weight_decay = 0.01
adam_eps = 1e-08
norm_eps = 1e-05

ROWS = 720
CH = 144
NCH = 5
PR = 96
GR = 24
ORDER_P = (2, 1, 3, 0)
ORDER_Q = (2, 3, 1, 0)


def gather_taps(padded, row_count, col_count):
    taps = [
        padded[:, row_off : row_off + row_count, col_off : col_off + col_count, :]
        for row_off in range(3)
        for col_off in range(3)
    ]
    return jnp.concatenate(taps, axis=3)


def adam(master, first_moment, second_moment, gradient):
    first_moment = beta_one * first_moment + (1.0 - beta_one) * gradient
    second_moment = beta_two * second_moment + (1.0 - beta_two) * gradient * gradient
    first_hat = first_moment / (1.0 - beta_one**step_count)
    second_hat = second_moment / (1.0 - beta_two**step_count)
    master = master - learn_rate * (
        first_hat / (jnp.sqrt(second_hat) + adam_eps) + weight_decay * master
    )
    return (master, first_moment, second_moment)


def group_totals(values, image_count, group_width):
    return jnp.sum(values, axis=(1, 2)).reshape(image_count, GROUPS, group_width).sum(-1)


def mod4(v):
    return lax.rem(v, 4)


def device(x, y, z, c):
    return ((mod4(z) * 4 + x) * 2 + c, y * 2 + lax.div(z, 4))


def piece_row(h, xq, y, zh):
    k = 4 * h + xq
    return pl.multiple_of(ROWS * (2 * y + zh) + PR * k - 48 * lax.div(k, 7), 16)


def exchange_kernel(
    w_ref, st_ref, wg_ref, W, ST, G,
    RX, R1R, R1L, R2R, R2L, S1R, S1L, S2R, S2L, D, Z,
    x_s, x_r, t_s, t_r, z_s, z_r, g_s, g_r, y_s, y_r, c_s, c_r, l_s,
):
    r = lax.axis_index("rep")
    s = lax.axis_index("shard")
    c = lax.rem(r, 2)
    x = mod4(lax.div(r, 2))
    zl = lax.div(r, 8)
    zh = lax.rem(s, 2)
    y = lax.div(s, 2)
    z = zh * 4 + zl
    p = x + c * (y - x)
    q = y + c * (x - y)
    sib = device(x, y, z, 1 - c)
    xr = device(mod4(x + 1), y, z, c)
    xl = device(mod4(x + 3), y, z, c)
    r1 = device(mod4(x + 1 - c), mod4(y + c), z, c)
    l1 = device(mod4(x + 3 * (1 - c)), mod4(y + 3 * c), z, c)
    r2 = device(mod4(x + c), mod4(y + 1 - c), z, c)
    l2 = device(mod4(x + 3 * c), mod4(y + 3 * (1 - c)), z, c)
    zpeer = [device(x, y, lax.rem(z + d, 8), c) for d in range(8)]
    lpeer = [device(x, y, zh * 4 + mod4(zl + d), c) for d in range(4)]
    sends = []

    def send(src, dst, ssem, rsem, dev):
        copy = pltpu.make_async_remote_copy(
            src_ref=src, dst_ref=dst, send_sem=ssem, recv_sem=rsem, device_id=dev, device_id_type=MESH
        )
        copy.start()
        return copy

    def post(*args):
        sends.append(send(*args))

    def arrived(dst, rsem):
        pltpu.make_async_remote_copy(
            src_ref=dst, dst_ref=dst, send_sem=l_s.at[1], recv_sem=rsem, device_id=sib, device_id_type=MESH
        ).wait_recv()

    barrier = pltpu.get_barrier_semaphore()
    peers = [sib, xr, xl, device(x, mod4(y + 1), z, c), device(x, mod4(y + 3), z, c)] + zpeer[1:]
    for peer in peers:
        pl.semaphore_signal(barrier, inc=1, device_id=peer, device_id_type=MESH)
    pl.semaphore_wait(barrier, len(peers))

    def gather_z(buf, src, ss, rs):
        for d in (2, 3, 1):
            post(src, buf.at[c, x, zl], ss.at[d - 1], rs.at[d - 1], lpeer[d])

    def gather_x(buf, ss, rs):
        for d in (2, 3, 1):
            arrived(buf.at[c, x, mod4(zl + 4 - d)], rs.at[d - 1])
        mine = buf.at[c, x]
        post(mine, mine, ss.at[3], rs.at[3], xr)
        post(mine, mine, ss.at[4], rs.at[4], xl)
        post(mine, mine, ss.at[7], rs.at[7], sib)

    def gather_relay(buf, ss, rs):
        left, right = mod4(x + 3), mod4(x + 1)
        arrived(buf.at[c, left], rs.at[3])
        half = buf.at[c, left, pl.ds(0, 2)]
        post(half, half, ss.at[5], rs.at[5], xr)
        post(buf.at[c, left], buf.at[c, left], ss.at[8], rs.at[8], sib)
        arrived(buf.at[c, right], rs.at[4])
        half = buf.at[c, right, pl.ds(2, 2)]
        post(half, half, ss.at[6], rs.at[6], xl)
        post(buf.at[c, right], buf.at[c, right], ss.at[9], rs.at[9], sib)

    def gather_end(buf, ss, rs):
        far = mod4(x + 2)
        arrived(buf.at[c, far, pl.ds(0, 2)], rs.at[5])
        arrived(buf.at[c, far, pl.ds(2, 2)], rs.at[6])
        post(buf.at[c, far], buf.at[c, far], ss.at[10], rs.at[10], sib)

    def gather_wait(buf, rs):
        for k, xx in ((7, x), (8, mod4(x + 3)), (9, mod4(x + 1)), (10, mod4(x + 2))):
            arrived(buf.at[1 - c, xx], rs.at[k])

    y_next, y_prev = mod4(y + 1 + 2 * c), mod4(y + 3 - 2 * c)
    y_far = mod4(y + 2)
    ynd = device(x, y_next, z, c)
    znd = device(x, y, lax.rem(z + 1 + 6 * c, 8), c)
    last = (1 - c) * lax.div(zl, 3) + c * (1 - lax.div(zl + 2, 3))
    order_z = (mod4(y + c), mod4(y + 3 - c))

    def wchunk(yy, hh, k):
        return W.at[pl.ds(pl.multiple_of(ROWS * (2 * yy + hh) + CH * k, 16), CH)]

    own = pltpu.make_async_copy(w_ref, W.at[pl.ds(pl.multiple_of(ROWS * s, 16), ROWS)], l_s.at[0])
    own.start()
    for k in range(NCH):
        post(w_ref.at[pl.ds(CH * k, CH)], wchunk(y, zh, k), y_s.at[k], y_r.at[k], ynd)
    own.wait()

    def weights_y():
        for k in range(NCH):
            chunk = wchunk(y_prev, zh, k)
            arrived(chunk, y_r.at[k])
            post(chunk, chunk, c_s.at[k], c_r.at[k], sib)
        for i in range(2):
            chunk = wchunk(y_prev, zh, i + 3 * c)
            post(chunk, chunk, y_s.at[NCH + i], y_r.at[NCH + i], ynd)

        @pl.when(c == 0)
        def _():
            chunk = wchunk(y_prev, zh, 2)
            send(chunk, chunk, y_s.at[NCH + 2], y_r.at[NCH + 2], ynd)

    def weights_far():
        for i in range(2):
            chunk = wchunk(y_far, zh, i + 3 * c)
            arrived(chunk, y_r.at[NCH + i])
            post(chunk, chunk, c_s.at[NCH + i], c_r.at[NCH + i], sib)

        @pl.when(c == 0)
        def _():
            chunk = wchunk(y_far, zh, 2)
            arrived(chunk, y_r.at[NCH + 2])
            send(chunk, chunk, c_s.at[NCH + 2], c_r.at[NCH + 2], sib)

        other = y_next
        for k in range(NCH):
            arrived(wchunk(other, zh, k), c_r.at[k])
        for i in range(2):
            arrived(wchunk(y_far, zh, i + 3 * (1 - c)), c_r.at[NCH + i])

        @pl.when(c == 1)
        def _():
            arrived(wchunk(y_far, zh, 2), c_r.at[NCH + 2])

    def weights_z(i):
        m = order_z[i]
        for k in range(NCH):
            n = i * NCH + k
            out = wchunk(m, zh + (1 - last) * (1 - 2 * zh), k)
            into = wchunk(m, 1 - zh, k)
            ss, rs = z_s.at[8 + n], z_r.at[8 + n]

            @pl.when(last == 1)
            def _():
                send(out, out, ss, rs, znd)

            arrived(into, rs)

            @pl.when(last == 0)
            def _():
                send(out, out, ss, rs, znd)

            post(into, into, c_s.at[8 + n], c_r.at[8 + n], sib)

    def weights_wait():
        for i, m in enumerate((mod4(y + 1 - c), mod4(y + 2 + c))):
            for k in range(NCH):
                arrived(wchunk(m, 1 - zh, k), c_r.at[8 + i * NCH + k])
        for n in range(2 * NCH):
            chunk = wchunk(0, 0, 0)
            pltpu.make_async_remote_copy(
                src_ref=chunk, dst_ref=chunk, send_sem=z_s.at[8 + n], recv_sem=z_r.at[8 + n],
                device_id=znd, device_id_type=MESH,
            ).wait_send()

        @pl.when(c == 0)
        def _():
            for ss in (y_s.at[NCH + 2], c_s.at[NCH + 2]):
                chunk = wchunk(0, 0, 0)
                pltpu.make_async_remote_copy(
                    src_ref=chunk, dst_ref=chunk, send_sem=ss, recv_sem=z_r.at[8],
                    device_id=sib, device_id_type=MESH,
                ).wait_send()

    cs = 1 - c
    ps = x + cs * (y - x)
    qs = y + cs * (x - y)
    for di, d in enumerate(ORDER_P):
        for oi, o in enumerate(ORDER_Q):
            a, b = mod4(ps + d), mod4(qs + o)
            xq, yy = a + cs * (b - a), b + cs * (a - b)
            for zz in range(2):
                n = di * 8 + oi * 2 + zz
                post(wg_ref.at[pl.ds(piece_row(cs, xq, yy, zz), PR)], RX.at[a, b, zz], x_s.at[n], x_r.at[n], sib)

    def chip_sum(di, oi, zz, extra=(), into=None):
        a, b = mod4(p + ORDER_P[di]), mod4(q + ORDER_Q[oi])
        xq, yy = a + c * (b - a), b + c * (a - b)
        row = piece_row(c, xq, yy, zz)
        arrived(RX.at[a, b, zz], x_r.at[di * 8 + oi * 2 + zz])
        if into is None:

            def body(i, carry):
                k = pl.multiple_of(i * 16, 16)
                total = RX[a, b, zz, pl.ds(k, 16), :].astype(F32) + wg_ref[pl.ds(row + k, 16), :].astype(F32)
                for ref in extra:
                    total = total + ref[pl.ds(k, 16), :].astype(F32)
                RX[a, b, zz, pl.ds(k, 16), :] = total.astype(BF16)
                return carry

            lax.fori_loop(0, PR // 16, body, 0)
        else:
            total = RX[a, b, zz].astype(F32) + wg_ref[pl.ds(row, PR), :].astype(F32)
            for ref in extra:
                total = total + ref[...].astype(F32)
            for g in range(4):
                into[zz, g] = total[GR * g : GR * (g + 1)].astype(BF16)
        return a, b

    mine_st = pltpu.make_async_copy(st_ref, ST.at[c, x, zl], l_s.at[1])
    mine_st.start()
    gather_z(ST, st_ref, t_s, t_r)
    mine_st.wait()

    for oi in range(4):
        a, b = chip_sum(0, oi, 0)
        post(RX.at[a, b, 0], R1R.at[oi], g_s.at[oi], g_r.at[oi], r1)
        chip_sum(0, oi, 1)
        post(RX.at[a, b, 1], R1L.at[oi], g_s.at[4 + oi], g_r.at[4 + oi], l1)
    weights_y()
    gather_x(ST, t_s, t_r)
    for oi in range(4):
        arrived(R1R.at[oi], g_r.at[oi])
        a, b = chip_sum(1, oi, 0, (R1R.at[oi],))
        chip_sum(1, oi, 1)
        post(RX.at[a, b], R2R.at[oi], g_s.at[8 + oi], g_r.at[8 + oi], r1)
        arrived(R1L.at[oi], g_r.at[4 + oi])
        chip_sum(2, oi, 0)
        a, b = chip_sum(2, oi, 1, (R1L.at[oi],))
        post(RX.at[a, b], R2L.at[oi], g_s.at[12 + oi], g_r.at[12 + oi], l1)
    weights_z(0)
    gather_relay(ST, t_s, t_r)
    weights_far()
    for oi in range(4):
        arrived(R2R.at[oi], g_r.at[8 + oi])
        arrived(R2L.at[oi], g_r.at[12 + oi])
        extra = [[R2R.at[oi, zz], R2L.at[oi, zz]] for zz in range(2)]
        if oi == 1:
            arrived(S1L, g_r.at[17])
            extra[1].append(S1L)
        if oi == 2:
            arrived(S1R, g_r.at[16])
            extra[0].append(S1R)
        if oi == 3:
            arrived(S2R, g_r.at[18])
            arrived(S2L, g_r.at[19])
            extra[0] += [S2R.at[0], S2L.at[0]]
            extra[1] += [S2R.at[1], S2L.at[1]]
        for zz in range(2):
            a, b = chip_sum(3, oi, zz, extra[zz], D if oi == 3 else None)
        if oi == 0:
            post(RX.at[a, b, 0], S1R, g_s.at[16], g_r.at[16], r2)
            post(RX.at[a, b, 1], S1L, g_s.at[17], g_r.at[17], l2)
        if oi == 1:
            post(RX.at[a, b], S2L, g_s.at[19], g_r.at[19], l2)
        if oi == 2:
            post(RX.at[a, b], S2R, g_s.at[18], g_r.at[18], r2)
    for d in (4, 3, 5, 2, 6, 1, 7):
        zz = lax.rem(z + d, 8)
        post(D.at[lax.div(zz, 4), mod4(zz)], Z.at[d], z_s.at[d], z_r.at[d], zpeer[d])
    gather_end(ST, t_s, t_r)
    weights_z(1)
    total = D[zh, zl].astype(F32)
    for d in (1, 7, 2, 6, 3, 5, 4):
        arrived(Z.at[d], z_r.at[d])
        total = total + Z[d].astype(F32)
    G[c, x, zl] = total.astype(BF16)
    gather_z(G, G.at[c, x, zl], t_s.at[pl.ds(11, 11)], t_r.at[pl.ds(11, 11)])
    gather_x(G, t_s.at[pl.ds(11, 11)], t_r.at[pl.ds(11, 11)])
    gather_relay(G, t_s.at[pl.ds(11, 11)], t_r.at[pl.ds(11, 11)])
    gather_end(G, t_s.at[pl.ds(11, 11)], t_r.at[pl.ds(11, 11)])
    gather_wait(ST, t_r)
    weights_wait()
    gather_wait(G, t_r.at[pl.ds(11, 11)])
    for copy in sends:
        copy.wait_send()


def exchange(weight, states, grads):
    dma = pltpu.SemaphoreType.DMA
    half = pltpu.VMEM((PR, 640), BF16)
    return pl.pallas_call(
        exchange_kernel,
        out_shape=(
            jax.ShapeDtypeStruct((8 * ROWS, 640), BF16),
            jax.ShapeDtypeStruct((2, 4, 4) + states.shape, BF16),
            jax.ShapeDtypeStruct((2, 4, 4, GR, 640), BF16),
        ),
        in_specs=[pl.BlockSpec(memory_space=pltpu.VMEM)] * 3,
        out_specs=[pl.BlockSpec(memory_space=pltpu.VMEM)] * 3,
        scratch_shapes=[
            pltpu.VMEM((4, 4, 2, PR, 640), BF16),
            pltpu.VMEM((4, PR, 640), BF16),
            pltpu.VMEM((4, PR, 640), BF16),
            pltpu.VMEM((4, 2, PR, 640), BF16),
            pltpu.VMEM((4, 2, PR, 640), BF16),
            half,
            half,
            pltpu.VMEM((2, PR, 640), BF16),
            pltpu.VMEM((2, PR, 640), BF16),
            pltpu.VMEM((2, 4, GR, 640), BF16),
            pltpu.VMEM((8, GR, 640), BF16),
            dma((32,)), dma((32,)),
            dma((22,)), dma((22,)),
            dma((18,)), dma((18,)),
            dma((20,)), dma((20,)),
            dma((8,)), dma((8,)),
            dma((18,)), dma((18,)),
            dma((2,)),
        ],
        compiler_params=pltpu.CompilerParams(
            collective_id=0, has_side_effects=True, vmem_limit_bytes=60 * 1024 * 1024
        ),
        name="exchange",
    )(weight, states, grads)


def per_device(
    latents,
    cotangent,
    gn_gain,
    gn_bias,
    conv_weight,
    master,
    moment_one,
    moment_two,
    departing,
    partner,
):
    image_count, row_count, col_count, channels = latents.shape
    group_width = channels // GROUPS
    pixel_count = row_count * col_count * group_width
    float_in = latents.astype(jnp.float32)
    group_mean = group_totals(float_in, image_count, group_width) / pixel_count
    centred = float_in - jnp.repeat(group_mean, group_width, axis=1)[:, None, None, :]
    variance = group_totals(centred * centred, image_count, group_width) / pixel_count
    inverse = jnp.repeat(lax.rsqrt(variance + norm_eps), group_width, axis=1)[:, None, None, :]
    activated = jax.nn.silu(centred * inverse * gn_gain + gn_bias).astype(jnp.bfloat16)
    padded = jnp.pad(activated, ((0, 0), (1, 1), (1, 1), (0, 0)))
    patches = gather_taps(padded, row_count, col_count).reshape(-1, 9 * channels)
    out_cols = conv_weight.shape[1]
    my_index = lax.axis_index("rep")
    staying = (1 - departing[my_index]).astype(jnp.float32)
    partner_index = partner[my_index]
    block_cols = master.shape[0]
    cot_flat = cotangent.reshape(-1, out_cols)
    terms = lax.dot_general(
        patches, cot_flat, (((0,), (0,)), ((), ())), preferred_element_type=jnp.float32
    )
    terms = (terms * staying).astype(BF16)
    states = jnp.stack([master, moment_one, moment_two]).astype(BF16).reshape(3 * block_cols, ROWS)
    weight, gathered, grads = exchange(conv_weight, states, terms)
    forward = jnp.dot(patches, weight, preferred_element_type=jnp.float32)
    conv_out = forward.astype(jnp.bfloat16).reshape(image_count, row_count, col_count, out_cols)

    rows = grads.reshape(8 * PR, out_cols)
    rows = jnp.concatenate([rows[: 7 * PR], rows[7 * PR + 48 :]])
    columns = lax.broadcasted_iota(jnp.int32, (2 * block_cols, out_cols), 1)
    slots = lax.broadcasted_iota(jnp.int32, (2 * block_cols, out_cols), 0)
    wanted = jnp.where(
        slots < block_cols, my_index * block_cols + slots, (partner_index - 1) * block_cols + slots
    )
    picked = lax.dot_general(
        (columns == wanted).astype(BF16), rows, (((1,), (1,)), ((), ())), preferred_element_type=F32
    )
    picked = picked / (image_count * lax.axis_size("shard") * (lax.axis_size("rep") // 2))
    slot = (lax.rem(partner_index, 2) * 4 + lax.rem(partner_index // 2, 4)) * 4 + partner_index // 8
    mate = lax.dynamic_index_in_dim(
        gathered.reshape(32, 3, block_cols, ROWS), slot, 0, keepdims=False
    ).astype(F32)
    own_state = adam(master, moment_one, moment_two, picked[:block_cols])
    mate_state = adam(mate[0], mate[1], mate[2], picked[block_cols:])

    def arrange(own_part, mate_part):
        return (jnp.stack([own_part, mate_part]) * staying)[None]

    return (
        conv_out,
        arrange(own_state[0], mate_state[0]),
        arrange(own_state[1], mate_state[1]),
        arrange(own_state[2], mate_state[2]),
    )


def solution(mesh):
    return jax.shard_map(
        per_device,
        mesh=mesh,
        in_specs=(
            P(("rep", "shard"), None, None, None),
            P(("rep", "shard"), None, None, None),
            P(),
            P(),
            P("shard", None),
            P("rep", "shard"),
            P("rep", "shard"),
            P("rep", "shard"),
            P(),
            P(),
        ),
        out_specs=(
            P(("rep", "shard"), None, None, None),
            P("rep", None, None, "shard"),
            P("rep", None, None, "shard"),
            P("rep", None, None, "shard"),
        ),
        check_vma=False,
    )
```

```python
import jax
import jax.numpy as jnp
from jax import lax
from jax.experimental import pallas as pl
from jax.experimental.pallas import tpu as pltpu
from jax.sharding import PartitionSpec as P

GROUPS = 32
MESH = pl.DeviceIdType.MESH
F32 = jnp.float32
BF16 = jnp.bfloat16

beta_one = 0.9
beta_two = 0.999
step_count = 100.0
learn_rate = 0.01
weight_decay = 0.01
adam_eps = 1e-08
norm_eps = 1e-05

ROWS = 720
CH = 144
NCH = 5
TM = 480
PR = 96
GR = 24
ORDER_P = (2, 1, 3, 0)
ORDER_Q = (2, 3, 1, 0)


def adam(master, first_moment, second_moment, gradient):
    first_moment = beta_one * first_moment + (1.0 - beta_one) * gradient
    second_moment = beta_two * second_moment + (1.0 - beta_two) * gradient * gradient
    first_hat = first_moment / (1.0 - beta_one**step_count)
    second_hat = second_moment / (1.0 - beta_two**step_count)
    master = master - learn_rate * (
        first_hat / (jnp.sqrt(second_hat) + adam_eps) + weight_decay * master
    )
    return (master, first_moment, second_moment)


def group_totals(values, image_count, group_width):
    return jnp.sum(values, axis=(1, 2)).reshape(image_count, GROUPS, group_width).sum(-1)


def mod4(v):
    return lax.rem(v, 4)


def device(x, y, z, c):
    return ((mod4(z) * 4 + x) * 2 + c, y * 2 + lax.div(z, 4))


def piece_row(h, xq, y, zh):
    k = 4 * h + xq
    return pl.multiple_of(ROWS * (2 * y + zh) + PR * k - 48 * lax.div(k, 7), 16)


def exchange_kernel(
    act_ref, act_t_ref, cot_ref, w_ref, st_ref, OUT, ST, G,
    W, WG, ACC, RX, R1R, R1L, R2R, R2L, S1R, S1L, S2R, S2L, D, Z,
    x_s, x_r, t_s, t_r, h_s, h_r, z_s, z_r, g_s, g_r, y_s, y_r, c_s, c_r, l_s,
):
    r = lax.axis_index("rep")
    s = lax.axis_index("shard")
    c = lax.rem(r, 2)
    x = mod4(lax.div(r, 2))
    zl = lax.div(r, 8)
    zh = lax.rem(s, 2)
    y = lax.div(s, 2)
    z = zh * 4 + zl
    p = x + c * (y - x)
    q = y + c * (x - y)
    sib = device(x, y, z, 1 - c)
    xpeer = [device(mod4(x + d), y, z, c) for d in range(4)]
    ypeer = [device(x, mod4(y + d), z, c) for d in range(4)]
    r1 = device(mod4(x + 1 - c), mod4(y + c), z, c)
    l1 = device(mod4(x + 3 * (1 - c)), mod4(y + 3 * c), z, c)
    r2 = device(mod4(x + c), mod4(y + 1 - c), z, c)
    l2 = device(mod4(x + 3 * c), mod4(y + 3 * (1 - c)), z, c)
    zpeer = [device(x, y, lax.rem(z + d, 8), c) for d in range(8)]
    lpeer = [device(x, y, zh * 4 + mod4(zl + d), c) for d in range(4)]
    sends = []

    def send(src, dst, ssem, rsem, dev):
        copy = pltpu.make_async_remote_copy(
            src_ref=src, dst_ref=dst, send_sem=ssem, recv_sem=rsem, device_id=dev, device_id_type=MESH
        )
        copy.start()
        return copy

    def post(*args):
        sends.append(send(*args))

    def arrived(dst, rsem):
        pltpu.make_async_remote_copy(
            src_ref=dst, dst_ref=dst, send_sem=l_s.at[0], recv_sem=rsem, device_id=sib, device_id_type=MESH
        ).wait_recv()

    def sent(src, ssem):
        pltpu.make_async_remote_copy(
            src_ref=src, dst_ref=src, send_sem=ssem, recv_sem=x_r.at[0], device_id=sib, device_id_type=MESH
        ).wait_send()

    own = pltpu.make_async_copy(w_ref, W.at[pl.ds(pl.multiple_of(ROWS * s, 16), ROWS)], l_s.at[0])
    own.start()
    mine_st = pltpu.make_async_copy(st_ref, ST.at[c, x, zl], l_s.at[1])
    mine_st.start()
    barrier = pltpu.get_barrier_semaphore()
    peers = [sib] + xpeer[1:] + ypeer[1:] + zpeer[1:]
    for peer in peers:
        pl.semaphore_signal(barrier, inc=1, device_id=peer, device_id_type=MESH)
    own.wait()
    mine_st.wait()
    pl.semaphore_wait(barrier, len(peers))

    def gather_z(buf, ss, rs):
        for d in (2, 3, 1):
            post(buf.at[c, x, zl], buf.at[c, x, zl], ss.at[d - 1], rs.at[d - 1], lpeer[d])

    def gather_x(buf, ss, rs):
        for d in (2, 3, 1):
            arrived(buf.at[c, x, mod4(zl + 4 - d)], rs.at[d - 1])
        mine = buf.at[c, x]
        for d in (2, 1, 3):
            post(mine, mine, ss.at[2 + d], rs.at[2 + d], xpeer[d])
        post(mine, mine, ss.at[6], rs.at[6], sib)

    def gather_end(buf, ss, rs):
        for d in (1, 3, 2):
            part = buf.at[c, mod4(x + 4 - d)]
            arrived(part, rs.at[2 + d])
            post(part, part, ss.at[6 + d], rs.at[6 + d], sib)

    def gather_wait(buf, rs):
        for d in range(4):
            arrived(buf.at[1 - c, mod4(x + 4 - d)], rs.at[6 + d])

    up = mod4(y + 3 - 2 * c)
    far = mod4(y + 2)
    ynd = device(x, mod4(y + 1 + 2 * c), z, c)
    znd = device(x, y, lax.rem(z + 1 + 6 * c, 8), c)
    last = (1 - c) * lax.div(zl, 3) + c * (1 - lax.div(zl + 2, 3))

    def wchunk(yy, hh, k):
        return W.at[pl.ds(pl.multiple_of(ROWS * (2 * yy + hh) + CH * k, 16), CH)]

    def entry(n, cc):
        if n < 2:
            return y, n + 3 * cc
        if n < 7:
            return mod4(y + 3 - 2 * cc), n - 2
        if n < 9:
            return far, n - 7 + 2 * cc
        return mod4(y + 2 * cc), 2 + 2 * cc

    def z_first(n):
        @pl.when(last == 1)
        def _():
            m, k = entry(n, c)
            send(wchunk(m, zh, k), wchunk(m, zh, k), z_s.at[8 + n], z_r.at[8 + n], znd)

    def weights_start():
        for k in range(NCH):
            post(wchunk(y, zh, k), wchunk(y, zh, k), y_s.at[k], y_r.at[k], ynd)
        for n in range(2):
            z_first(n)
        for i in range(2):
            chunk = wchunk(y, zh, i + 2 * c)
            post(chunk, chunk, y_s.at[NCH + i], y_r.at[NCH + i], ypeer[2])

        @pl.when(c == 1)
        def _():
            chunk = wchunk(y, zh, 4)
            send(chunk, chunk, y_s.at[NCH + 2], y_r.at[NCH + 2], ypeer[2])

    def weights_y(k):
        chunk = wchunk(up, zh, k)
        arrived(chunk, y_r.at[k])
        z_first(2 + k)
        post(chunk, chunk, c_s.at[k], c_r.at[k], sib)

    def weights_far():
        for i in range(2):
            chunk = wchunk(far, zh, i + 2 * c)
            arrived(chunk, y_r.at[NCH + i])
            z_first(7 + i)
            post(chunk, chunk, c_s.at[NCH + i], c_r.at[NCH + i], sib)

        @pl.when(c == 1)
        def _():
            chunk = wchunk(far, zh, 4)
            arrived(chunk, y_r.at[NCH + 2])
            send(chunk, chunk, c_s.at[NCH + 2], c_r.at[NCH + 2], sib)

        z_first(9)

    def weights_z(n):
        m, k = entry(n, c)
        chunk = wchunk(m, 1 - zh, k)
        arrived(chunk, z_r.at[8 + n])

        @pl.when(last == 0)
        def _():
            send(chunk, chunk, z_s.at[8 + n], z_r.at[8 + n], znd)

        post(chunk, chunk, c_s.at[8 + n], c_r.at[8 + n], sib)

    def weights_wait():
        cs = 1 - c
        for k in range(NCH):
            arrived(wchunk(mod4(y + 3 - 2 * cs), zh, k), c_r.at[k])
        for i in range(2):
            arrived(wchunk(far, zh, i + 2 * cs), c_r.at[NCH + i])

        @pl.when(c == 0)
        def _():
            arrived(wchunk(far, zh, 4), c_r.at[NCH + 2])

        for n in range(10):
            m, k = entry(n, cs)
            arrived(wchunk(m, 1 - zh, k), c_r.at[8 + n])

    def weights_sent():
        for n in range(10):
            sent(wchunk(0, 0, 0), z_s.at[8 + n])

        @pl.when(c == 1)
        def _():
            sent(wchunk(0, 0, 0), y_s.at[NCH + 2])
            sent(wchunk(0, 0, 0), c_s.at[NCH + 2])

    def terms(yy):
        def tile(i, carry):
            m = yy * 3 + i
            tap_row = lax.div(m, 4)
            lhs = act_t_ref[pl.ds(pl.multiple_of(TM * mod4(m), 16), TM), :]
            rhs = cot_ref[pl.ds(pl.multiple_of(32 * (2 - tap_row), 32), 1024), :]
            WG[pl.ds(pl.multiple_of(TM * m, 16), TM), :] = jnp.dot(
                lhs, rhs, preferred_element_type=F32
            ).astype(BF16)
            return carry

        lax.fori_loop(0, 3, tile, 0)

    def pair_send(yy):
        cs = 1 - c
        for xq in range(4):
            a, b = xq + cs * (yy - xq), yy + cs * (xq - yy)
            for zz in range(2):
                n = (xq * 4 + yy) * 2 + zz
                post(WG.at[pl.ds(piece_row(cs, xq, yy, zz), PR)], RX.at[a, b, zz], x_s.at[n], x_r.at[n], sib)

    def chip_sum(di, oi, zz, extra=(), into=None):
        a, b = mod4(p + ORDER_P[di]), mod4(q + ORDER_Q[oi])
        xq, yy = a + c * (b - a), b + c * (a - b)
        row = piece_row(c, xq, yy, zz)
        arrived(RX.at[a, b, zz], x_r.at[(xq * 4 + yy) * 2 + zz])
        if into is None:

            def body(i, carry):
                k = pl.multiple_of(i * 16, 16)
                total = RX[a, b, zz, pl.ds(k, 16), :].astype(F32) + WG[pl.ds(row + k, 16), :].astype(F32)
                for ref in extra:
                    total = total + ref[pl.ds(k, 16), :].astype(F32)
                RX[a, b, zz, pl.ds(k, 16), :] = total.astype(BF16)
                return carry

            lax.fori_loop(0, PR // 16, body, 0)
        else:
            total = RX[a, b, zz].astype(F32) + WG[pl.ds(row, PR), :].astype(F32)
            for ref in extra:
                total = total + ref[...].astype(F32)
            for g in range(4):
                into[zz, g] = total[GR * g : GR * (g + 1)].astype(BF16)
        return a, b

    def conv(a):
        def tile(i, carry):
            at = pl.ds(pl.multiple_of(256 * i, 256), 256)
            lhs = act_ref[pl.ds(pl.multiple_of(256 * i + 32 * a, 32), 256), :]
            total = jnp.dot(lhs, W[1920 * a : 1920 * (a + 1), :], preferred_element_type=F32)
            if a > 0:
                total = total + ACC[at, :]
            if a < 2:
                ACC[at, :] = total
            else:
                OUT[at, :] = total.astype(BF16)
            return carry

        lax.fori_loop(0, 4, tile, 0)

    weights_start()
    gather_z(ST, t_s, t_r)
    terms(0)
    pair_send(0)
    weights_y(0)
    terms(1)
    pair_send(1)
    weights_y(1)
    weights_z(0)
    terms(2)
    pair_send(2)
    weights_y(2)
    weights_z(1)
    gather_x(ST, t_s, t_r)
    terms(3)
    pair_send(3)
    for oi in range(4):
        a, b = chip_sum(0, oi, 0)
        post(RX.at[a, b, 0], R1R.at[oi], g_s.at[oi], g_r.at[oi], r1)
        chip_sum(0, oi, 1)
        post(RX.at[a, b, 1], R1L.at[oi], g_s.at[4 + oi], g_r.at[4 + oi], l1)
    weights_y(3)
    weights_y(4)
    weights_z(2)
    weights_z(3)
    for oi in range(4):
        arrived(R1R.at[oi], g_r.at[oi])
        a, b = chip_sum(1, oi, 0, (R1R.at[oi],))
        chip_sum(1, oi, 1)
        post(RX.at[a, b], R2R.at[oi], g_s.at[8 + oi], g_r.at[8 + oi], r1)
        arrived(R1L.at[oi], g_r.at[4 + oi])
        chip_sum(2, oi, 0)
        a, b = chip_sum(2, oi, 1, (R1L.at[oi],))
        post(RX.at[a, b], R2L.at[oi], g_s.at[12 + oi], g_r.at[12 + oi], l1)
        if oi == 1:
            weights_far()
        if oi >= 1:
            weights_z(3 + oi)
    gather_end(ST, t_s, t_r)
    for oi in range(4):
        arrived(R2R.at[oi], g_r.at[8 + oi])
        arrived(R2L.at[oi], g_r.at[12 + oi])
        extra = [[R2R.at[oi, zz], R2L.at[oi, zz]] for zz in range(2)]
        if oi == 1:
            arrived(S1L, g_r.at[17])
            extra[1].append(S1L)
        if oi == 2:
            arrived(S1R, g_r.at[16])
            extra[0].append(S1R)
        if oi == 3:
            arrived(S2R, g_r.at[18])
            arrived(S2L, g_r.at[19])
            extra[0] += [S2R.at[0], S2L.at[0]]
            extra[1] += [S2R.at[1], S2L.at[1]]
        for zz in range(2):
            a, b = chip_sum(3, oi, zz, extra[zz], D if oi == 3 else None)
        if oi == 0:
            post(RX.at[a, b, 0], S1R, g_s.at[16], g_r.at[16], r2)
            post(RX.at[a, b, 1], S1L, g_s.at[17], g_r.at[17], l2)
        if oi == 1:
            post(RX.at[a, b], S2L, g_s.at[19], g_r.at[19], l2)
        if oi == 2:
            post(RX.at[a, b], S2R, g_s.at[18], g_r.at[18], r2)
        if oi < 3:
            weights_z(7 + oi)
    for d in (4, 3, 5, 2, 6, 1, 7):
        zz = lax.rem(z + d, 8)
        post(D.at[lax.div(zz, 4), mod4(zz)], Z.at[d], z_s.at[d], z_r.at[d], zpeer[d])
    weights_wait()
    conv(0)
    total = D[zh, zl].astype(F32)
    for d in (1, 7, 2, 6, 3, 5, 4):
        arrived(Z.at[d], z_r.at[d])
        total = total + Z[d].astype(F32)
    G[c, x, zl] = total.astype(BF16)
    gather_z(G, h_s, h_r)
    conv(1)
    gather_x(G, h_s, h_r)
    conv(2)
    gather_end(G, h_s, h_r)
    gather_wait(ST, t_r)
    weights_sent()
    gather_wait(G, h_r)
    for copy in sends:
        copy.wait_send()


def exchange(act, act_t, cot, weight, states):
    dma = pltpu.SemaphoreType.DMA
    half = pltpu.VMEM((PR, 640), BF16)
    return pl.pallas_call(
        exchange_kernel,
        out_shape=(
            jax.ShapeDtypeStruct((1024, 640), BF16),
            jax.ShapeDtypeStruct((2, 4, 4) + states.shape, BF16),
            jax.ShapeDtypeStruct((2, 4, 4, GR, 640), BF16),
        ),
        in_specs=[pl.BlockSpec(memory_space=pltpu.VMEM)] * 5,
        out_specs=[pl.BlockSpec(memory_space=pltpu.VMEM)] * 3,
        scratch_shapes=[
            pltpu.VMEM((8 * ROWS, 640), BF16),
            pltpu.VMEM((8 * ROWS, 640), BF16),
            pltpu.VMEM((1024, 640), F32),
            pltpu.VMEM((4, 4, 2, PR, 640), BF16),
            pltpu.VMEM((4, PR, 640), BF16),
            pltpu.VMEM((4, PR, 640), BF16),
            pltpu.VMEM((4, 2, PR, 640), BF16),
            pltpu.VMEM((4, 2, PR, 640), BF16),
            half,
            half,
            pltpu.VMEM((2, PR, 640), BF16),
            pltpu.VMEM((2, PR, 640), BF16),
            pltpu.VMEM((2, 4, GR, 640), BF16),
            pltpu.VMEM((8, GR, 640), BF16),
            dma((32,)), dma((32,)),
            dma((10,)), dma((10,)),
            dma((10,)), dma((10,)),
            dma((18,)), dma((18,)),
            dma((20,)), dma((20,)),
            dma((8,)), dma((8,)),
            dma((18,)), dma((18,)),
            dma((2,)),
        ],
        compiler_params=pltpu.CompilerParams(
            collective_id=0, has_side_effects=True, vmem_limit_bytes=60 * 1024 * 1024
        ),
        name="exchange",
    )(act, act_t, cot, weight, states)


def per_device(
    latents,
    cotangent,
    gn_gain,
    gn_bias,
    conv_weight,
    master,
    moment_one,
    moment_two,
    departing,
    partner,
):
    image_count, row_count, col_count, channels = latents.shape
    group_width = channels // GROUPS
    pixel_count = row_count * col_count * group_width
    float_in = latents.astype(jnp.float32)
    group_mean = group_totals(float_in, image_count, group_width) / pixel_count
    centred = float_in - jnp.repeat(group_mean, group_width, axis=1)[:, None, None, :]
    variance = group_totals(centred * centred, image_count, group_width) / pixel_count
    inverse = jnp.repeat(lax.rsqrt(variance + norm_eps), group_width, axis=1)[:, None, None, :]
    activated = jax.nn.silu(centred * inverse * gn_gain + gn_bias).astype(jnp.bfloat16)
    out_cols = conv_weight.shape[1]
    my_index = lax.axis_index("rep")
    staying = (1 - departing[my_index]).astype(jnp.float32)
    partner_index = partner[my_index]
    block_cols = master.shape[0]
    wide = jnp.pad(activated[0], ((0, 0), (1, 1), (0, 0)))
    shifted = jnp.concatenate([wide[:, b : b + col_count] for b in range(3)], axis=2)
    shifted = shifted.reshape(row_count * col_count, 3 * channels)
    act = jnp.pad(shifted, ((col_count, col_count), (0, 0)))
    cot = cotangent.reshape(-1, out_cols) * staying.astype(BF16)
    cot = jnp.pad(cot, ((col_count, col_count), (0, 0)))
    states = jnp.stack([master, moment_one, moment_two]).astype(BF16).reshape(3 * block_cols, ROWS)
    forward, gathered, grads = exchange(act, shifted.T, cot, conv_weight, states)
    conv_out = forward.reshape(image_count, row_count, col_count, out_cols)

    rows = grads.reshape(8 * PR, out_cols)
    rows = jnp.concatenate([rows[: 7 * PR], rows[7 * PR + 48 :]])
    columns = lax.broadcasted_iota(jnp.int32, (2 * block_cols, out_cols), 1)
    slots = lax.broadcasted_iota(jnp.int32, (2 * block_cols, out_cols), 0)
    wanted = jnp.where(
        slots < block_cols, my_index * block_cols + slots, (partner_index - 1) * block_cols + slots
    )
    picked = lax.dot_general(
        (columns == wanted).astype(BF16), rows, (((1,), (1,)), ((), ())), preferred_element_type=F32
    )
    picked = picked / (image_count * lax.axis_size("shard") * (lax.axis_size("rep") // 2))
    slot = (lax.rem(partner_index, 2) * 4 + lax.rem(partner_index // 2, 4)) * 4 + partner_index // 8
    mate = lax.dynamic_index_in_dim(
        gathered.reshape(32, 3 * block_cols, ROWS), slot, 0, keepdims=False
    )
    mate = mate.reshape(3, block_cols, ROWS).astype(F32)
    own_state = adam(master, moment_one, moment_two, picked[:block_cols])
    mate_state = adam(mate[0], mate[1], mate[2], picked[block_cols:])

    def arrange(own_part, mate_part):
        return (jnp.stack([own_part, mate_part]) * staying)[None]

    return (
        conv_out,
        arrange(own_state[0], mate_state[0]),
        arrange(own_state[1], mate_state[1]),
        arrange(own_state[2], mate_state[2]),
    )


def solution(mesh):
    return jax.shard_map(
        per_device,
        mesh=mesh,
        in_specs=(
            P(("rep", "shard"), None, None, None),
            P(("rep", "shard"), None, None, None),
            P(),
            P(),
            P("shard", None),
            P("rep", "shard"),
            P("rep", "shard"),
            P("rep", "shard"),
            P(),
            P(),
        ),
        out_specs=(
            P(("rep", "shard"), None, None, None),
            P("rep", None, None, "shard"),
            P("rep", None, None, "shard"),
            P("rep", None, None, "shard"),
        ),
        check_vma=False,
    )
```

```python
import jax
import jax.numpy as jnp
from jax import lax
from jax.experimental import pallas as pl
from jax.experimental.pallas import tpu as pltpu
from jax.sharding import PartitionSpec as P

GROUPS = 32
WIDTH = 20
MESH = pl.DeviceIdType.MESH
F32 = jnp.float32
BF16 = jnp.bfloat16
EXACT = lax.Precision.HIGHEST

beta_one = 0.9
beta_two = 0.999
step_count = 100.0
learn_rate = 0.01
weight_decay = 0.01
adam_eps = 1e-08
norm_eps = 1e-05

PIX = 1024
ROWS = 720
COLS = 20
CH = 144
NCH = 5
TM = 480
PR = 96
GR = 24
ORDER_P = (2, 1, 3, 0)
ORDER_Q = (2, 3, 1, 0)


def adam(master, first_moment, second_moment, gradient):
    first_moment = beta_one * first_moment + (1.0 - beta_one) * gradient
    second_moment = beta_two * second_moment + (1.0 - beta_two) * gradient * gradient
    first_hat = first_moment / (1.0 - beta_one**step_count)
    second_hat = second_moment / (1.0 - beta_two**step_count)
    master = master - learn_rate * (
        first_hat / (jnp.sqrt(second_hat) + adam_eps) + weight_decay * master
    )
    return (master, first_moment, second_moment)


def group_totals(values, image_count, group_width):
    return jnp.sum(values, axis=(1, 2)).reshape(image_count, GROUPS, group_width).sum(-1)


def mod4(v):
    return lax.rem(v, 4)


def device(x, y, z, c):
    return ((mod4(z) * 4 + x) * 2 + c, y * 2 + lax.div(z, 4))


def piece_row(h, xq, y, zh):
    k = 4 * h + xq
    return pl.multiple_of(ROWS * (2 * y + zh) + PR * k - 48 * lax.div(k, 7), 16)


def exchange_kernel(
    x_ref, cot_ref, gain_ref, bias_ref, w_ref, ma_ref, m1_ref, m2_ref, dep_ref, par_ref,
    OUT, NMA, NM1, NM2,
    ACT, ACT_T, COT, W, WG, ACC, RX, R1R, R1L, R2R, R2L, S1R, S1L, S2R, S2L, D, Z,
    SF, COL, SB, RB, GA, SEL, SG, RG, PLACE,
    x_s, x_r, t_s, t_r, h_s, h_r, z_s, z_r, g_s, g_r, y_s, y_r, c_s, c_r, l_s,
):
    r = lax.axis_index("rep")
    s = lax.axis_index("shard")
    c = lax.rem(r, 2)
    x = mod4(lax.div(r, 2))
    zl = lax.div(r, 8)
    zh = lax.rem(s, 2)
    y = lax.div(s, 2)
    z = zh * 4 + zl
    p = x + c * (y - x)
    q = y + c * (x - y)
    sib = device(x, y, z, 1 - c)
    xpeer = [device(mod4(x + d), y, z, c) for d in range(4)]
    ypeer = [device(x, mod4(y + d), z, c) for d in range(4)]
    r1 = device(mod4(x + 1 - c), mod4(y + c), z, c)
    l1 = device(mod4(x + 3 * (1 - c)), mod4(y + 3 * c), z, c)
    r2 = device(mod4(x + c), mod4(y + 1 - c), z, c)
    l2 = device(mod4(x + 3 * c), mod4(y + 3 * (1 - c)), z, c)
    zpeer = [device(x, y, lax.rem(z + d, 8), c) for d in range(8)]
    lpeer = [device(x, y, zh * 4 + mod4(zl + d), c) for d in range(4)]
    sends = []

    def send(src, dst, ssem, rsem, dev):
        copy = pltpu.make_async_remote_copy(
            src_ref=src, dst_ref=dst, send_sem=ssem, recv_sem=rsem, device_id=dev, device_id_type=MESH
        )
        copy.start()
        return copy

    def post(*args):
        sends.append(send(*args))

    def arrived(dst, rsem):
        pltpu.make_async_remote_copy(
            src_ref=dst, dst_ref=dst, send_sem=l_s.at[0], recv_sem=rsem, device_id=sib, device_id_type=MESH
        ).wait_recv()

    def sent(src, ssem):
        pltpu.make_async_remote_copy(
            src_ref=src, dst_ref=src, send_sem=ssem, recv_sem=x_r.at[0], device_id=sib, device_id_type=MESH
        ).wait_send()

    own = pltpu.make_async_copy(w_ref, W.at[pl.ds(pl.multiple_of(ROWS * s, 16), ROWS)], l_s.at[0])
    own.start()
    cots = pltpu.make_async_copy(cot_ref, COT.at[pl.ds(32, PIX)], l_s.at[1])
    cots.start()
    barrier = pltpu.get_barrier_semaphore()
    peers = [sib] + xpeer[1:] + ypeer[1:] + zpeer[1:]
    for peer in peers:
        pl.semaphore_signal(barrier, inc=1, device_id=peer, device_id_type=MESH)
    staying = (1 - dep_ref[r]).astype(F32)

    SF[...] = jnp.zeros_like(SF)
    for n, ref in enumerate((ma_ref, m1_ref, m2_ref)):
        SF[GR * n : GR * n + COLS, :] = ref[...]
    COL[c, zl] = SF[...].astype(BF16)

    chan = lax.broadcasted_iota(jnp.int32, (640, 128), 0)
    low = lax.broadcasted_iota(jnp.int32, (640, 128), 1) * WIDTH
    member = ((chan >= low) & (chan < low + WIDTH)).astype(F32)
    chan = lax.broadcasted_iota(jnp.int32, (128, 640), 1)
    low = lax.broadcasted_iota(jnp.int32, (128, 640), 0) * WIDTH
    spread = ((chan >= low) & (chan < low + WIDTH)).astype(F32)

    def group_mean(sums):
        sums = jnp.broadcast_to(jnp.sum(sums, axis=0, keepdims=True), (8, 640))
        sums = jnp.dot(sums, member, preferred_element_type=F32, precision=EXACT)
        sums = jnp.dot(sums, spread, preferred_element_type=F32, precision=EXACT)
        return sums[0:1] * (1.0 / (PIX * WIDTH))

    def tile_of(i):
        return x_ref[pl.ds(pl.multiple_of(i * 64, 64), 64), :].astype(F32)

    def add_tile(i, sums):
        return sums + jnp.sum(tile_of(i).reshape(8, 8, 640), axis=0)

    mean = group_mean(lax.fori_loop(0, PIX // 64, add_tile, jnp.zeros((8, 640), F32)))

    def add_square(i, sums):
        centred = tile_of(i) - mean
        return sums + jnp.sum((centred * centred).reshape(8, 8, 640), axis=0)

    variance = group_mean(lax.fori_loop(0, PIX // 64, add_square, jnp.zeros((8, 640), F32)))
    scale = lax.rsqrt(variance + norm_eps) * gain_ref[...]

    own.wait()
    pl.semaphore_wait(barrier, len(peers))

    def gather_z(buf, ss, rs):
        for d in (2, 3, 1):
            post(buf.at[c, zl], buf.at[c, zl], ss.at[d - 1], rs.at[d - 1], lpeer[d])

    def gather_pair(buf, ss, rs):
        for d in (2, 3, 1):
            arrived(buf.at[c, mod4(zl + 4 - d)], rs.at[d - 1])
        post(buf.at[c], buf.at[c], ss.at[3], rs.at[3], sib)

    def rep_at(d):
        return (zl * 4 + mod4(x + d)) * 2 + c

    def states_select():
        arrived(COL.at[1 - c], t_r.at[3])
        for d in range(4):
            mate = par_ref[rep_at(d)]
            block = COL[lax.rem(mate, 2), lax.div(mate, 8)]
            if d == 0:
                RB[0] = block
            else:
                SB[d - 1] = block
                post(SB.at[d - 1], RB.at[d], t_s.at[3 + d], t_r.at[3 + d], xpeer[d])

    def columns_prepare():
        slot = lax.broadcasted_iota(jnp.int32, (48, 640), 0)
        col = lax.broadcasted_iota(jnp.int32, (48, 640), 1)
        for d in range(4):
            rep = rep_at(d)
            base = jnp.where(slot < GR, rep * COLS, par_ref[rep] * COLS - GR) + slot
            SEL[48 * d : 48 * (d + 1), :] = (col == base).astype(F32).astype(BF16)
        row = lax.broadcasted_iota(jnp.int32, (2 * PR, ROWS), 0)
        col = lax.broadcasted_iota(jnp.int32, (2 * PR, ROWS), 1)
        for d in range(4):
            xs = mod4(x + 4 - d)
            dup = 48 * lax.div(xs, 3)
            base = row + PR * xs + jnp.where(row < PR, 0, 3 * PR - dup)
            keep = (row < PR) | (row >= PR + dup)
            PLACE[d] = ((col == base) & keep).astype(F32).astype(BF16)

    def columns_select():
        arrived(GA.at[1 - c], h_r.at[3])
        rows = GA[...].astype(F32).reshape(2 * PR, 640).astype(BF16)
        picked = lax.dot_general(
            SEL[...], rows, (((1,), (1,)), ((), ())), preferred_element_type=F32
        ).astype(BF16)
        RG[0] = picked[0:48]
        for d in range(1, 4):
            SG[d - 1] = picked[48 * d : 48 * (d + 1)]
            post(SG.at[d - 1], RG.at[d], h_s.at[3 + d], h_r.at[3 + d], xpeer[d])

    def optimize():
        picked = jnp.dot(RG[0], PLACE[0], preferred_element_type=F32)
        for d in (1, 3, 2):
            arrived(RG.at[d], h_r.at[3 + d])
            arrived(RB.at[d], t_r.at[3 + d])
            picked = picked + jnp.dot(RG[d], PLACE[d], preferred_element_type=F32)
        picked = picked * (1.0 / 128.0)
        mate = par_ref[r]
        block = RB[lax.rem(x + 4 - mod4(lax.div(mate, 2)), 4)].astype(F32)
        held = [ref[...] for ref in (ma_ref, m1_ref, m2_ref)]
        mates = [block[GR * n : GR * n + COLS] for n in range(3)]
        for n, state, grad in ((0, held, picked[0:COLS]), (1, mates, picked[GR : GR + COLS])):
            for ref, value in zip((NMA, NM1, NM2), adam(*state, grad)):
                ref[n] = value * staying

    up = mod4(y + 3 - 2 * c)
    far = mod4(y + 2)
    ynd = device(x, mod4(y + 1 + 2 * c), z, c)
    znd = device(x, y, lax.rem(z + 1 + 6 * c, 8), c)

    def wchunk(yy, hh, k):
        return W.at[pl.ds(pl.multiple_of(ROWS * (2 * yy + hh) + CH * k, 16), CH)]

    pos = (1 - c) * zl + c * (3 - zl)
    last = lax.div(pos, 3)

    def entry(n, cc):
        v = n + 3 * cc + 2 * lax.div(n + 7 - 4 * cc, 10)
        t = lax.div(v, 5)
        return mod4(y + 8 + t * (3 - 2 * cc) + lax.div(t * (t - 1), 2) * (4 * cc - 4)), lax.rem(v, 5)

    def z_send(n):
        m, k = entry(n, c)
        send(wchunk(m, zh, k), wchunk(m, zh, k), z_s.at[8 + n], z_r.at[8 + n], znd)

    def weights_start():
        for k in range(NCH):
            post(wchunk(y, zh, k), wchunk(y, zh, k), y_s.at[k], y_r.at[k], ynd)

        @pl.when(last == 1)
        def _():
            z_send(0)
            z_send(1)

        @pl.when((last == 1) & (c == 0))
        def _():
            z_send(2)

    def weights_y(k):
        chunk = wchunk(up, zh, k)
        arrived(chunk, y_r.at[k])

        @pl.when(c == (0 if k < 2 else 1))
        def _():
            send(chunk, chunk, y_s.at[NCH + k], y_r.at[NCH + k], ynd)

        @pl.when(last == 1)
        def _():
            z_send(3 + k - c)

        post(chunk, chunk, c_s.at[k], c_r.at[k], sib)

    def weights_far():
        for k in range(NCH):

            @pl.when(c == (0 if k < 2 else 1))
            def _():
                chunk = wchunk(far, zh, k)
                arrived(chunk, y_r.at[NCH + k])
                send(chunk, chunk, c_s.at[NCH + k], c_r.at[NCH + k], sib)

        @pl.when(last == 1)
        def _():
            z_send(8)
            z_send(9)

        @pl.when((last == 1) & (c == 1))
        def _():
            z_send(7)

    def weights_z(slot):
        n = slot - pos

        @pl.when((n >= 0) & (n < 10))
        def _():
            m, k = entry(n, c)
            chunk = wchunk(m, 1 - zh, k)
            arrived(chunk, z_r.at[8 + n])

            @pl.when(last == 0)
            def _():
                send(chunk, chunk, z_s.at[8 + n], z_r.at[8 + n], znd)

            send(chunk, chunk, c_s.at[10 + n], c_r.at[10 + n], sib)

    def weights_wait():
        cs = 1 - c
        for k in range(NCH):
            arrived(wchunk(mod4(y + 3 - 2 * cs), zh, k), c_r.at[k])

            @pl.when(c == (1 if k < 2 else 0))
            def _():
                arrived(wchunk(far, zh, k), c_r.at[NCH + k])

        for n in range(10):
            m, k = entry(n, cs)
            arrived(wchunk(m, 1 - zh, k), c_r.at[10 + n])

    def weights_sent():
        for n in range(10):
            sent(wchunk(0, 0, 0), z_s.at[8 + n])
            sent(wchunk(0, 0, 0), c_s.at[10 + n])
        for k in range(NCH):

            @pl.when(c == (0 if k < 2 else 1))
            def _():
                sent(wchunk(0, 0, 0), y_s.at[NCH + k])
                sent(wchunk(0, 0, 0), c_s.at[NCH + k])

    def terms(yy):
        def tile(i, carry):
            m = yy * 3 + i
            tap_row = lax.div(m, 4)
            lhs = ACT_T[pl.ds(pl.multiple_of(TM * mod4(m), 16), TM), :]
            rhs = COT[pl.ds(pl.multiple_of(32 * (2 - tap_row), 32), PIX), :]
            product = jnp.dot(lhs, rhs, preferred_element_type=F32)
            WG[pl.ds(pl.multiple_of(TM * m, 16), TM), :] = (product * staying).astype(BF16)
            return carry

        lax.fori_loop(0, 3, tile, 0)

    def pair_send(yy):
        cs = 1 - c
        for xq in range(4):
            a, b = xq + cs * (yy - xq), yy + cs * (xq - yy)
            for zz in range(2):
                n = (xq * 4 + yy) * 2 + zz
                post(WG.at[pl.ds(piece_row(cs, xq, yy, zz), PR)], RX.at[a, b, zz], x_s.at[n], x_r.at[n], sib)

    def chip_sum(di, oi, zz, extra=(), into=None):
        a, b = mod4(p + ORDER_P[di]), mod4(q + ORDER_Q[oi])
        xq, yy = a + c * (b - a), b + c * (a - b)
        row = piece_row(c, xq, yy, zz)
        arrived(RX.at[a, b, zz], x_r.at[(xq * 4 + yy) * 2 + zz])
        if into is None:

            def body(i, carry):
                k = pl.multiple_of(i * 16, 16)
                total = RX[a, b, zz, pl.ds(k, 16), :].astype(F32) + WG[pl.ds(row + k, 16), :].astype(F32)
                for ref in extra:
                    total = total + ref[pl.ds(k, 16), :].astype(F32)
                RX[a, b, zz, pl.ds(k, 16), :] = total.astype(BF16)
                return carry

            lax.fori_loop(0, PR // 16, body, 0)
        else:
            total = RX[a, b, zz].astype(F32) + WG[pl.ds(row, PR), :].astype(F32)
            for ref in extra:
                total = total + ref[...].astype(F32)
            for g in range(4):
                into[zz, g] = total[GR * g : GR * (g + 1)].astype(BF16)
        return a, b

    def conv(a):
        def tile(i, carry):
            at = pl.ds(pl.multiple_of(256 * i, 256), 256)
            lhs = ACT[pl.ds(pl.multiple_of(256 * i + 32 * a, 32), 256), :]
            total = jnp.dot(lhs, W[1920 * a : 1920 * (a + 1), :], preferred_element_type=F32)
            if a > 0:
                total = total + ACC[at, :]
            if a < 2:
                ACC[at, :] = total
            else:
                OUT[at, :] = total.astype(BF16)
            return carry

        lax.fori_loop(0, 4, tile, 0)

    weights_start()
    gather_z(COL, t_s, t_r)

    edge = jnp.zeros((32, 1920), BF16)
    ACT[0:32, :] = edge
    ACT[PIX + 32 : PIX + 64, :] = edge
    COT[0:32, :] = edge[:, 0:640]
    COT[PIX + 32 : PIX + 64, :] = edge[:, 0:640]

    def activate(i, carry):
        value = x_ref[pl.ds(pl.multiple_of(i * 128, 128), 128), :].astype(F32)
        value = (value - mean) * scale + bias_ref[...]
        value = value * (0.5 * jnp.tanh(0.5 * value) + 0.5)
        column = lax.broadcasted_iota(jnp.int32, (128, 640), 0) & 31
        for b in range(3):
            if b == 0:
                part = jnp.where(column == 0, 0.0, pltpu.roll(value, 1, 0))
            elif b == 1:
                part = value
            else:
                part = jnp.where(column == 31, 0.0, pltpu.roll(value, 127, 0))
            ACT[pl.ds(pl.multiple_of(i * 128 + 32, 32), 128), 640 * b : 640 * (b + 1)] = part.astype(BF16)
            ACT_T[640 * b : 640 * (b + 1), pl.ds(pl.multiple_of(i * 128, 128), 128)] = part.T.astype(BF16)
        return carry

    lax.fori_loop(0, PIX // 128, activate, 0)
    cots.wait()
    terms(0)
    pair_send(0)
    weights_y(0)
    weights_z(0)
    terms(1)
    pair_send(1)
    weights_y(1)
    weights_y(2)
    weights_z(1)
    gather_pair(COL, t_s, t_r)
    terms(2)
    pair_send(2)
    weights_y(3)
    weights_z(2)
    terms(3)
    pair_send(3)
    weights_y(4)
    weights_z(3)
    for oi in range(4):
        a, b = chip_sum(0, oi, 0)
        post(RX.at[a, b, 0], R1R.at[oi], g_s.at[oi], g_r.at[oi], r1)
        chip_sum(0, oi, 1)
        post(RX.at[a, b, 1], R1L.at[oi], g_s.at[4 + oi], g_r.at[4 + oi], l1)
    weights_z(4)
    states_select()
    columns_prepare()
    for oi in range(4):
        arrived(R1R.at[oi], g_r.at[oi])
        a, b = chip_sum(1, oi, 0, (R1R.at[oi],))
        chip_sum(1, oi, 1)
        post(RX.at[a, b], R2R.at[oi], g_s.at[8 + oi], g_r.at[8 + oi], r1)
        arrived(R1L.at[oi], g_r.at[4 + oi])
        chip_sum(2, oi, 0)
        a, b = chip_sum(2, oi, 1, (R1L.at[oi],))
        post(RX.at[a, b], R2L.at[oi], g_s.at[12 + oi], g_r.at[12 + oi], l1)
        if oi == 0:
            weights_far()
        weights_z(5 + oi)
    for oi in range(4):
        arrived(R2R.at[oi], g_r.at[8 + oi])
        arrived(R2L.at[oi], g_r.at[12 + oi])
        extra = [[R2R.at[oi, zz], R2L.at[oi, zz]] for zz in range(2)]
        if oi == 1:
            arrived(S1L, g_r.at[17])
            extra[1].append(S1L)
        if oi == 2:
            arrived(S1R, g_r.at[16])
            extra[0].append(S1R)
        if oi == 3:
            arrived(S2R, g_r.at[18])
            arrived(S2L, g_r.at[19])
            extra[0] += [S2R.at[0], S2L.at[0]]
            extra[1] += [S2R.at[1], S2L.at[1]]
        for zz in range(2):
            a, b = chip_sum(3, oi, zz, extra[zz], D if oi == 3 else None)
        if oi == 0:
            post(RX.at[a, b, 0], S1R, g_s.at[16], g_r.at[16], r2)
            post(RX.at[a, b, 1], S1L, g_s.at[17], g_r.at[17], l2)
        if oi == 1:
            post(RX.at[a, b], S2L, g_s.at[19], g_r.at[19], l2)
        if oi == 2:
            post(RX.at[a, b], S2R, g_s.at[18], g_r.at[18], r2)
        weights_z(9 + oi)
    for d in (4, 3, 5, 2, 6, 1, 7):
        zz = lax.rem(z + d, 8)
        post(D.at[lax.div(zz, 4), mod4(zz)], Z.at[d], z_s.at[d], z_r.at[d], zpeer[d])
    weights_wait()
    conv(0)
    total = D[zh, zl].astype(F32)
    for d in (1, 7, 2, 6, 3, 5, 4):
        arrived(Z.at[d], z_r.at[d])
        total = total + Z[d].astype(F32)
    GA[c, zl] = total.astype(BF16)
    gather_z(GA, h_s, h_r)
    conv(1)
    gather_pair(GA, h_s, h_r)
    columns_select()
    conv(2)
    optimize()
    weights_sent()
    for copy in sends:
        copy.wait_send()


def exchange(latents, cotangent, gain, bias, weight, master, moment_one, moment_two, departing, partner):
    dma = pltpu.SemaphoreType.DMA
    vmem, smem = pl.BlockSpec(memory_space=pltpu.VMEM), pl.BlockSpec(memory_space=pltpu.SMEM)
    anywhere = pl.BlockSpec(memory_space=pl.ANY)
    half = pltpu.VMEM((PR, 640), BF16)
    state = jax.ShapeDtypeStruct((2, COLS, ROWS), F32)
    return pl.pallas_call(
        exchange_kernel,
        out_shape=(jax.ShapeDtypeStruct((PIX, 640), BF16), state, state, state),
        in_specs=[vmem, anywhere, vmem, vmem, anywhere, vmem, vmem, vmem, smem, smem],
        out_specs=[vmem] * 4,
        scratch_shapes=[
            pltpu.VMEM((PIX + 64, 1920), BF16),
            pltpu.VMEM((1920, PIX), BF16),
            pltpu.VMEM((PIX + 64, 640), BF16),
            pltpu.VMEM((8 * ROWS, 640), BF16),
            pltpu.VMEM((8 * ROWS, 640), BF16),
            pltpu.VMEM((PIX, 640), F32),
            pltpu.VMEM((4, 4, 2, PR, 640), BF16),
            pltpu.VMEM((4, PR, 640), BF16),
            pltpu.VMEM((4, PR, 640), BF16),
            pltpu.VMEM((4, 2, PR, 640), BF16),
            pltpu.VMEM((4, 2, PR, 640), BF16),
            half,
            half,
            pltpu.VMEM((2, PR, 640), BF16),
            pltpu.VMEM((2, PR, 640), BF16),
            pltpu.VMEM((2, 4, GR, 640), BF16),
            pltpu.VMEM((8, GR, 640), BF16),
            pltpu.VMEM((3 * GR, ROWS), F32),
            pltpu.VMEM((2, 4, 3 * GR, ROWS), BF16),
            pltpu.VMEM((3, 3 * GR, ROWS), BF16),
            pltpu.VMEM((4, 3 * GR, ROWS), BF16),
            pltpu.VMEM((2, 4, GR, 640), BF16),
            pltpu.VMEM((4 * 48, 640), BF16),
            pltpu.VMEM((3, 48, 2 * PR), BF16),
            pltpu.VMEM((4, 48, 2 * PR), BF16),
            pltpu.VMEM((4, 2 * PR, ROWS), BF16),
            dma((32,)), dma((32,)),
            dma((7,)), dma((7,)),
            dma((7,)), dma((7,)),
            dma((18,)), dma((18,)),
            dma((20,)), dma((20,)),
            dma((10,)), dma((10,)),
            dma((20,)), dma((20,)),
            dma((2,)),
        ],
        compiler_params=pltpu.CompilerParams(
            collective_id=0, has_side_effects=True, vmem_limit_bytes=60 * 1024 * 1024
        ),
        name="exchange",
    )(latents, cotangent, gain, bias, weight, master, moment_one, moment_two, departing, partner)


def per_device(
    latents,
    cotangent,
    gn_gain,
    gn_bias,
    conv_weight,
    master,
    moment_one,
    moment_two,
    departing,
    partner,
):
    forward, new_master, new_first, new_second = exchange(
        latents.reshape(PIX, -1),
        cotangent.reshape(PIX, -1),
        gn_gain.reshape(1, -1),
        gn_bias.reshape(1, -1),
        conv_weight,
        master,
        moment_one,
        moment_two,
        departing,
        partner,
    )
    return forward.reshape(cotangent.shape), new_master[None], new_first[None], new_second[None]


def solution(mesh):
    return jax.shard_map(
        per_device,
        mesh=mesh,
        in_specs=(
            P(("rep", "shard"), None, None, None),
            P(("rep", "shard"), None, None, None),
            P(),
            P(),
            P("shard", None),
            P("rep", "shard"),
            P("rep", "shard"),
            P("rep", "shard"),
            P(),
            P(),
        ),
        out_specs=(
            P(("rep", "shard"), None, None, None),
            P("rep", None, None, "shard"),
            P("rep", None, None, "shard"),
            P("rep", None, None, "shard"),
        ),
        check_vma=False,
    )
```

```python
import jax
import jax.numpy as jnp
from jax import lax
from jax.experimental import pallas as pl
from jax.experimental.pallas import tpu as pltpu
from jax.sharding import PartitionSpec as P

GROUPS = 32
WIDTH = 20
MESH = pl.DeviceIdType.MESH
F32 = jnp.float32
BF16 = jnp.bfloat16
EXACT = lax.Precision.HIGHEST

beta_one = 0.9
beta_two = 0.999
step_count = 100.0
learn_rate = 0.01
weight_decay = 0.01
adam_eps = 1e-08
norm_eps = 1e-05

PIX = 1024
ROWS = 720
COLS = 20
CH = 144
NCH = 5
TM = 480
PR = 96
LAG = 2
GR = 24
ORDER_P = (2, 1, 3, 0)
ORDER_Q = (2, 3, 1, 0)


def adam(master, first_moment, second_moment, gradient):
    first_moment = beta_one * first_moment + (1.0 - beta_one) * gradient
    second_moment = beta_two * second_moment + (1.0 - beta_two) * gradient * gradient
    first_hat = first_moment / (1.0 - beta_one**step_count)
    second_hat = second_moment / (1.0 - beta_two**step_count)
    master = master - learn_rate * (
        first_hat / (jnp.sqrt(second_hat) + adam_eps) + weight_decay * master
    )
    return (master, first_moment, second_moment)


def group_totals(values, image_count, group_width):
    return jnp.sum(values, axis=(1, 2)).reshape(image_count, GROUPS, group_width).sum(-1)


def mod4(v):
    return lax.rem(v, 4)


def device(x, y, z, c):
    return ((mod4(z) * 4 + x) * 2 + c, y * 2 + lax.div(z, 4))


def piece_row(h, xq, y, zh):
    k = 4 * h + xq
    return pl.multiple_of(ROWS * (2 * y + zh) + PR * k - 48 * lax.div(k, 7), 16)


def exchange_kernel(
    x_ref, cot_ref, gain_ref, bias_ref, w_ref, ma_ref, m1_ref, m2_ref, dep_ref, par_ref,
    OUT, NMA, NM1, NM2,
    ACT, ACT_T, COT, W, WG, ACC, RX, R1R, R1L, R2R, R2L, S1R, S1L, S2R, S2L, D, Z,
    SF, COL, SB, RB, GA, SEL, SG, RG, PLACE,
    x_s, x_r, t_s, t_r, h_s, h_r, z_s, z_r, g_s, g_r, y_s, y_r, c_s, c_r, l_s,
):
    r = lax.axis_index("rep")
    s = lax.axis_index("shard")
    c = lax.rem(r, 2)
    x = mod4(lax.div(r, 2))
    zl = lax.div(r, 8)
    zh = lax.rem(s, 2)
    y = lax.div(s, 2)
    z = zh * 4 + zl
    p = x + c * (y - x)
    q = y + c * (x - y)
    sib = device(x, y, z, 1 - c)
    xpeer = [device(mod4(x + d), y, z, c) for d in range(4)]
    ypeer = [device(x, mod4(y + d), z, c) for d in range(4)]
    r1 = device(mod4(x + 1 - c), mod4(y + c), z, c)
    l1 = device(mod4(x + 3 * (1 - c)), mod4(y + 3 * c), z, c)
    r2 = device(mod4(x + c), mod4(y + 1 - c), z, c)
    l2 = device(mod4(x + 3 * c), mod4(y + 3 * (1 - c)), z, c)
    zpeer = [device(x, y, lax.rem(z + d, 8), c) for d in range(8)]
    lpeer = [device(x, y, zh * 4 + mod4(zl + d), c) for d in range(4)]
    sends = []

    def send(src, dst, ssem, rsem, dev):
        copy = pltpu.make_async_remote_copy(
            src_ref=src, dst_ref=dst, send_sem=ssem, recv_sem=rsem, device_id=dev, device_id_type=MESH
        )
        copy.start()
        return copy

    def post(*args):
        sends.append(send(*args))

    def arrived(dst, rsem):
        pltpu.make_async_remote_copy(
            src_ref=dst, dst_ref=dst, send_sem=l_s.at[0], recv_sem=rsem, device_id=sib, device_id_type=MESH
        ).wait_recv()

    def sent(src, ssem):
        pltpu.make_async_remote_copy(
            src_ref=src, dst_ref=src, send_sem=ssem, recv_sem=x_r.at[0], device_id=sib, device_id_type=MESH
        ).wait_send()

    own = pltpu.make_async_copy(w_ref, W.at[pl.ds(pl.multiple_of(ROWS * s, 16), ROWS)], l_s.at[0])
    own.start()
    cots = pltpu.make_async_copy(cot_ref, COT.at[pl.ds(32, PIX)], l_s.at[1])
    cots.start()
    barrier = pltpu.get_barrier_semaphore()
    peers = [sib] + xpeer[1:] + ypeer[1:] + zpeer[1:]
    for peer in peers:
        pl.semaphore_signal(barrier, inc=1, device_id=peer, device_id_type=MESH)
    staying = (1 - dep_ref[r]).astype(F32)

    SF[...] = jnp.zeros_like(SF)
    for n, ref in enumerate((ma_ref, m1_ref, m2_ref)):
        SF[GR * n : GR * n + COLS, :] = ref[...]
    COL[c, zl] = SF[...].astype(BF16)

    chan = lax.broadcasted_iota(jnp.int32, (640, 128), 0)
    low = lax.broadcasted_iota(jnp.int32, (640, 128), 1) * WIDTH
    member = ((chan >= low) & (chan < low + WIDTH)).astype(F32)
    chan = lax.broadcasted_iota(jnp.int32, (128, 640), 1)
    low = lax.broadcasted_iota(jnp.int32, (128, 640), 0) * WIDTH
    spread = ((chan >= low) & (chan < low + WIDTH)).astype(F32)

    def group_mean(sums):
        sums = jnp.broadcast_to(jnp.sum(sums, axis=0, keepdims=True), (8, 640))
        sums = jnp.dot(sums, member, preferred_element_type=F32, precision=EXACT)
        sums = jnp.dot(sums, spread, preferred_element_type=F32, precision=EXACT)
        return sums[0:1] * (1.0 / (PIX * WIDTH))

    def tile_of(i):
        return x_ref[pl.ds(pl.multiple_of(i * 64, 64), 64), :].astype(F32)

    def add_tile(i, sums):
        return sums + jnp.sum(tile_of(i).reshape(8, 8, 640), axis=0)

    mean = group_mean(lax.fori_loop(0, PIX // 64, add_tile, jnp.zeros((8, 640), F32)))

    def add_square(i, sums):
        centred = tile_of(i) - mean
        return sums + jnp.sum((centred * centred).reshape(8, 8, 640), axis=0)

    variance = group_mean(lax.fori_loop(0, PIX // 64, add_square, jnp.zeros((8, 640), F32)))
    bias = bias_ref[...].reshape(1, 640)
    scale = lax.rsqrt(variance + norm_eps) * gain_ref[...].reshape(1, 640)

    own.wait()
    pl.semaphore_wait(barrier, len(peers))

    def gather_z(buf, ss, rs, steps=(2, 3, 1)):
        for d in steps:
            post(buf.at[c, zl], buf.at[c, zl], ss.at[d - 1], rs.at[d - 1], lpeer[d])

    def gather_pair(buf, ss, rs):
        for d in (2, 3, 1):
            arrived(buf.at[c, mod4(zl + 4 - d)], rs.at[d - 1])
        post(buf.at[c], buf.at[c], ss.at[3], rs.at[3], sib)

    def rep_at(d):
        return (zl * 4 + mod4(x + d)) * 2 + c

    def states_select():
        arrived(COL.at[1 - c], t_r.at[3])
        for d in range(4):
            mate = par_ref[rep_at(d)]
            block = COL[lax.rem(mate, 2), lax.div(mate, 8)]
            if d == 0:
                RB[0] = block
            else:
                SB[d - 1] = block
                post(SB.at[d - 1], RB.at[d], t_s.at[3 + d], t_r.at[3 + d], xpeer[d])

    def columns_prepare():
        slot = lax.broadcasted_iota(jnp.int32, (48, 640), 0)
        col = lax.broadcasted_iota(jnp.int32, (48, 640), 1)
        for d in range(4):
            rep = rep_at(d)
            base = jnp.where(slot < GR, rep * COLS, par_ref[rep] * COLS - GR) + slot
            SEL[48 * d : 48 * (d + 1), :] = (col == base).astype(F32).astype(BF16)
        row = lax.broadcasted_iota(jnp.int32, (2 * PR, ROWS), 0)
        col = lax.broadcasted_iota(jnp.int32, (2 * PR, ROWS), 1)
        for d in range(4):
            xs = mod4(x + 4 - d)
            dup = 48 * lax.div(xs, 3)
            base = row + PR * xs + jnp.where(row < PR, 0, 3 * PR - dup)
            keep = (row < PR) | (row >= PR + dup)
            PLACE[d] = ((col == base) & keep).astype(F32).astype(BF16)

    def columns_select():
        arrived(GA.at[1 - c], h_r.at[3])
        rows = GA[...].astype(F32).reshape(2 * PR, 640).astype(BF16)
        picked = lax.dot_general(
            SEL[...], rows, (((1,), (1,)), ((), ())), preferred_element_type=F32
        ).astype(BF16)
        RG[0] = picked[0:48]
        for d in range(1, 4):
            SG[d - 1] = picked[48 * d : 48 * (d + 1)]
            post(SG.at[d - 1], RG.at[d], h_s.at[3 + d], h_r.at[3 + d], xpeer[d])

    def optimize():
        picked = jnp.dot(RG[0], PLACE[0], preferred_element_type=F32)
        for d in (1, 3, 2):
            arrived(RG.at[d], h_r.at[3 + d])
            arrived(RB.at[d], t_r.at[3 + d])
            picked = picked + jnp.dot(RG[d], PLACE[d], preferred_element_type=F32)
        picked = picked * (1.0 / 128.0)
        mate = par_ref[r]
        block = RB[lax.rem(x + 4 - mod4(lax.div(mate, 2)), 4)].astype(F32)
        held = [ref[...] for ref in (ma_ref, m1_ref, m2_ref)]
        mates = [block[GR * n : GR * n + COLS] for n in range(3)]
        for n, state, grad in ((0, held, picked[0:COLS]), (1, mates, picked[GR : GR + COLS])):
            for ref, value in zip((NMA, NM1, NM2), adam(*state, grad)):
                ref[:, n, :] = value * staying

    up = mod4(y + 3 - 2 * c)
    far = mod4(y + 2)
    ynd = device(x, mod4(y + 1 + 2 * c), z, c)
    znd = device(x, y, lax.rem(z + 1 + 6 * c, 8), c)

    def wchunk(yy, hh, k):
        return W.at[pl.ds(pl.multiple_of(ROWS * (2 * yy + hh) + CH * k, 16), CH)]

    pos = (1 - c) * zl + c * (3 - zl)
    last = lax.div(pos, 3)

    def entry(n, cc):
        v = n + 3 * cc + 2 * lax.div(n + 7 - 4 * cc, 10)
        t = lax.div(v, 5)
        return mod4(y + 8 + t * (3 - 2 * cc) + lax.div(t * (t - 1), 2) * (4 * cc - 4)), lax.rem(v, 5)

    def z_send(n):
        m, k = entry(n, c)
        send(wchunk(m, zh, k), wchunk(m, zh, k), z_s.at[8 + n], z_r.at[8 + n], znd)

    def weights_start():
        for k in range(NCH):
            post(wchunk(y, zh, k), wchunk(y, zh, k), y_s.at[k], y_r.at[k], ynd)

        @pl.when(last == 1)
        def _():
            z_send(0)
            z_send(1)

        @pl.when((last == 1) & (c == 0))
        def _():
            z_send(2)

    def weights_y(k):
        chunk = wchunk(up, zh, k)
        arrived(chunk, y_r.at[k])

        @pl.when(c == (0 if k < 2 else 1))
        def _():
            send(chunk, chunk, y_s.at[NCH + k], y_r.at[NCH + k], ynd)

        @pl.when(last == 1)
        def _():
            z_send(3 + k - c)

        post(chunk, chunk, c_s.at[k], c_r.at[k], sib)

    def weights_far():
        for k in range(NCH):

            @pl.when(c == (0 if k < 2 else 1))
            def _():
                chunk = wchunk(far, zh, k)
                arrived(chunk, y_r.at[NCH + k])
                send(chunk, chunk, c_s.at[NCH + k], c_r.at[NCH + k], sib)

        @pl.when(last == 1)
        def _():
            z_send(8)
            z_send(9)

        @pl.when((last == 1) & (c == 1))
        def _():
            z_send(7)

    def weights_z(slot):
        n = slot - LAG * pos

        @pl.when((n >= 0) & (n < 10))
        def _():
            m, k = entry(n, c)
            chunk = wchunk(m, 1 - zh, k)
            arrived(chunk, z_r.at[8 + n])

            @pl.when(last == 0)
            def _():
                send(chunk, chunk, z_s.at[8 + n], z_r.at[8 + n], znd)

            send(chunk, chunk, c_s.at[10 + n], c_r.at[10 + n], sib)

    def weights_wait():
        cs = 1 - c
        for k in range(NCH):
            arrived(wchunk(mod4(y + 3 - 2 * cs), zh, k), c_r.at[k])

            @pl.when(c == (1 if k < 2 else 0))
            def _():
                arrived(wchunk(far, zh, k), c_r.at[NCH + k])

        for n in range(10):
            m, k = entry(n, cs)
            arrived(wchunk(m, 1 - zh, k), c_r.at[10 + n])

    def weights_sent():
        for n in range(10):
            sent(wchunk(0, 0, 0), z_s.at[8 + n])
            sent(wchunk(0, 0, 0), c_s.at[10 + n])
        for k in range(NCH):

            @pl.when(c == (0 if k < 2 else 1))
            def _():
                sent(wchunk(0, 0, 0), y_s.at[NCH + k])
                sent(wchunk(0, 0, 0), c_s.at[NCH + k])

    def terms(i, lo=0, hi=3):
        yy = mod4(y + ORDER_Q[i])

        def tile(k, carry):
            m = yy * 3 + k
            tap_row = lax.div(m, 4)
            lhs = ACT_T[pl.ds(pl.multiple_of(TM * mod4(m), 16), TM), :]
            rhs = COT[pl.ds(pl.multiple_of(32 * (2 - tap_row), 32), PIX), :]
            product = jnp.dot(lhs, rhs, preferred_element_type=F32)
            WG[pl.ds(pl.multiple_of(TM * m, 16), TM), :] = (product * staying).astype(BF16)
            return carry

        lax.fori_loop(lo, hi, tile, 0)

    def pair_send(i):
        cs = 1 - c
        yy = mod4(y + ORDER_Q[i])
        for xq in range(4):
            a, b = xq + cs * (yy - xq), yy + cs * (xq - yy)
            for zz in range(2):
                n = (xq * 4 + yy) * 2 + zz
                post(WG.at[pl.ds(piece_row(cs, xq, yy, zz), PR)], RX.at[a, b, zz], x_s.at[n], x_r.at[n], sib)

    def chip_sum(di, oi, zz, extra=(), into=None):
        a, b = mod4(p + ORDER_P[di]), mod4(q + ORDER_Q[oi])
        xq, yy = a + c * (b - a), b + c * (a - b)
        row = piece_row(c, xq, yy, zz)
        arrived(RX.at[a, b, zz], x_r.at[(xq * 4 + yy) * 2 + zz])
        if into is None:

            def body(i, carry):
                k = pl.multiple_of(i * 16, 16)
                total = RX[a, b, zz, pl.ds(k, 16), :].astype(F32) + WG[pl.ds(row + k, 16), :].astype(F32)
                for ref in extra:
                    total = total + ref[pl.ds(k, 16), :].astype(F32)
                RX[a, b, zz, pl.ds(k, 16), :] = total.astype(BF16)
                return carry

            lax.fori_loop(0, PR // 16, body, 0)
        else:
            total = RX[a, b, zz].astype(F32) + WG[pl.ds(row, PR), :].astype(F32)
            for ref in extra:
                total = total + ref[...].astype(F32)
            for g in range(4):
                into[zz, g] = total[GR * g : GR * (g + 1)].astype(BF16)
        return a, b

    def conv(a):
        def tile(i, carry):
            at = pl.ds(pl.multiple_of(256 * i, 256), 256)
            lhs = ACT[pl.ds(pl.multiple_of(256 * i + 32 * a, 32), 256), :]
            total = jnp.dot(lhs, W[1920 * a : 1920 * (a + 1), :], preferred_element_type=F32)
            if a > 0:
                total = total + ACC[at, :]
            if a < 2:
                ACC[at, :] = total
            else:
                OUT[at, :] = total.astype(BF16)
            return carry

        lax.fori_loop(0, 4, tile, 0)

    weights_start()
    gather_z(COL, t_s, t_r)

    edge = jnp.zeros((32, 1920), BF16)
    ACT[0:32, :] = edge
    ACT[PIX + 32 : PIX + 64, :] = edge
    COT[0:32, :] = edge[:, 0:640]
    COT[PIX + 32 : PIX + 64, :] = edge[:, 0:640]

    def activate(i, carry):
        value = x_ref[pl.ds(pl.multiple_of(i * 128, 128), 128), :].astype(F32)
        value = (value - mean) * scale + bias
        value = value * (0.5 * jnp.tanh(0.5 * value) + 0.5)
        column = lax.broadcasted_iota(jnp.int32, (128, 640), 0) & 31
        for b in range(3):
            if b == 0:
                part = jnp.where(column == 0, 0.0, pltpu.roll(value, 1, 0))
            elif b == 1:
                part = value
            else:
                part = jnp.where(column == 31, 0.0, pltpu.roll(value, 127, 0))
            ACT[pl.ds(pl.multiple_of(i * 128 + 32, 32), 128), 640 * b : 640 * (b + 1)] = part.astype(BF16)
            ACT_T[640 * b : 640 * (b + 1), pl.ds(pl.multiple_of(i * 128, 128), 128)] = part.T.astype(BF16)
        return carry

    lax.fori_loop(0, PIX // 128, activate, 0)
    cots.wait()
    def first_step(oi):
        a, b = chip_sum(0, oi, 0)
        post(RX.at[a, b, 0], R1R.at[oi], g_s.at[oi], g_r.at[oi], r1)
        chip_sum(0, oi, 1)
        post(RX.at[a, b, 1], R1L.at[oi], g_s.at[4 + oi], g_r.at[4 + oi], l1)

    def second_step(oi):
        arrived(R1R.at[oi], g_r.at[oi])
        a, b = chip_sum(1, oi, 0, (R1R.at[oi],))
        chip_sum(1, oi, 1)
        post(RX.at[a, b], R2R.at[oi], g_s.at[8 + oi], g_r.at[8 + oi], r1)
        arrived(R1L.at[oi], g_r.at[4 + oi])
        chip_sum(2, oi, 0)
        a, b = chip_sum(2, oi, 1, (R1L.at[oi],))
        post(RX.at[a, b], R2L.at[oi], g_s.at[12 + oi], g_r.at[12 + oi], l1)

    terms(0)
    pair_send(0)
    weights_y(0)
    weights_y(1)
    weights_z(0)
    terms(1, 0, 2)
    weights_z(1)
    terms(1, 2, 3)
    pair_send(1)
    first_step(0)
    weights_y(2)
    weights_y(3)
    weights_z(2)
    terms(2, 0, 2)
    weights_y(4)
    weights_z(3)
    terms(2, 2, 3)
    pair_send(2)
    first_step(1)
    weights_z(4)
    terms(3, 0, 2)
    weights_z(5)
    terms(3, 2, 3)
    pair_send(3)
    weights_far()
    weights_z(6)
    first_step(2)
    weights_z(7)
    first_step(3)
    weights_z(8)
    second_step(0)
    weights_z(9)
    gather_pair(COL, t_s, t_r)
    columns_prepare()
    second_step(1)
    weights_z(10)
    second_step(2)
    weights_z(11)
    second_step(3)
    weights_z(12)
    for oi in range(4):
        arrived(R2R.at[oi], g_r.at[8 + oi])
        arrived(R2L.at[oi], g_r.at[12 + oi])
        extra = [[R2R.at[oi, zz], R2L.at[oi, zz]] for zz in range(2)]
        if oi == 1:
            arrived(S1L, g_r.at[17])
            extra[1].append(S1L)
        if oi == 2:
            arrived(S1R, g_r.at[16])
            extra[0].append(S1R)
        if oi == 3:
            arrived(S2R, g_r.at[18])
            arrived(S2L, g_r.at[19])
            extra[0] += [S2R.at[0], S2L.at[0]]
            extra[1] += [S2R.at[1], S2L.at[1]]
        for zz in range(2):
            a, b = chip_sum(3, oi, zz, extra[zz], D if oi == 3 else None)
        if oi == 0:
            post(RX.at[a, b, 0], S1R, g_s.at[16], g_r.at[16], r2)
            post(RX.at[a, b, 1], S1L, g_s.at[17], g_r.at[17], l2)
        if oi == 1:
            post(RX.at[a, b], S2L, g_s.at[19], g_r.at[19], l2)
        if oi == 2:
            post(RX.at[a, b], S2R, g_s.at[18], g_r.at[18], r2)
        if oi < 3:
            weights_z(13 + oi)
    for d in (4, 3, 5, 2, 6, 1, 7):
        zz = lax.rem(z + d, 8)
        post(D.at[lax.div(zz, 4), mod4(zz)], Z.at[d], z_s.at[d], z_r.at[d], zpeer[d])
    weights_wait()
    conv(0)
    states_select()
    total = D[zh, zl].astype(F32)
    for d in (1, 7, 2, 6, 3, 5, 4):
        arrived(Z.at[d], z_r.at[d])
        total = total + Z[d].astype(F32)
    GA[c, zl] = total.astype(BF16)
    gather_z(GA, h_s, h_r)
    conv(1)
    gather_pair(GA, h_s, h_r)
    columns_select()
    conv(2)
    optimize()
    weights_sent()
    for copy in sends:
        copy.wait_send()


def exchange(latents, cotangent, gain, bias, weight, master, moment_one, moment_two, departing, partner):
    dma = pltpu.SemaphoreType.DMA
    vmem, smem = pl.BlockSpec(memory_space=pltpu.VMEM), pl.BlockSpec(memory_space=pltpu.SMEM)
    anywhere = pl.BlockSpec(memory_space=pl.ANY)
    half = pltpu.VMEM((PR, 640), BF16)
    state = jax.ShapeDtypeStruct((COLS, 2, ROWS), F32)
    return pl.pallas_call(
        exchange_kernel,
        out_shape=(jax.ShapeDtypeStruct((PIX, 640), BF16), state, state, state),
        in_specs=[vmem, anywhere, vmem, vmem, anywhere, vmem, vmem, vmem, smem, smem],
        out_specs=[vmem] * 4,
        scratch_shapes=[
            pltpu.VMEM((PIX + 64, 1920), BF16),
            pltpu.VMEM((1920, PIX), BF16),
            pltpu.VMEM((PIX + 64, 640), BF16),
            pltpu.VMEM((8 * ROWS, 640), BF16),
            pltpu.VMEM((8 * ROWS, 640), BF16),
            pltpu.VMEM((PIX, 640), F32),
            pltpu.VMEM((4, 4, 2, PR, 640), BF16),
            pltpu.VMEM((4, PR, 640), BF16),
            pltpu.VMEM((4, PR, 640), BF16),
            pltpu.VMEM((4, 2, PR, 640), BF16),
            pltpu.VMEM((4, 2, PR, 640), BF16),
            half,
            half,
            pltpu.VMEM((2, PR, 640), BF16),
            pltpu.VMEM((2, PR, 640), BF16),
            pltpu.VMEM((2, 4, GR, 640), BF16),
            pltpu.VMEM((8, GR, 640), BF16),
            pltpu.VMEM((3 * GR, ROWS), F32),
            pltpu.VMEM((2, 4, 3 * GR, ROWS), BF16),
            pltpu.VMEM((3, 3 * GR, ROWS), BF16),
            pltpu.VMEM((4, 3 * GR, ROWS), BF16),
            pltpu.VMEM((2, 4, GR, 640), BF16),
            pltpu.VMEM((4 * 48, 640), BF16),
            pltpu.VMEM((3, 48, 2 * PR), BF16),
            pltpu.VMEM((4, 48, 2 * PR), BF16),
            pltpu.VMEM((4, 2 * PR, ROWS), BF16),
            dma((32,)), dma((32,)),
            dma((7,)), dma((7,)),
            dma((7,)), dma((7,)),
            dma((18,)), dma((18,)),
            dma((20,)), dma((20,)),
            dma((10,)), dma((10,)),
            dma((20,)), dma((20,)),
            dma((2,)),
        ],
        compiler_params=pltpu.CompilerParams(
            collective_id=0, has_side_effects=True, vmem_limit_bytes=48 * 1024 * 1024
        ),
        name="exchange",
    )(latents, cotangent, gain, bias, weight, master, moment_one, moment_two, departing, partner)


def deliver_kernel(*refs):
    count = len(refs) // 2
    copies = [
        pltpu.make_async_copy(refs[n], refs[count + n], refs[-1].at[n]) for n in range(count)
    ]
    for copy in copies:
        copy.start()
    for copy in copies:
        copy.wait()


def deliver(*arrays):
    return pl.pallas_call(
        deliver_kernel,
        out_shape=tuple(jax.ShapeDtypeStruct(v.shape, v.dtype) for v in arrays),
        in_specs=[pl.BlockSpec(memory_space=pltpu.VMEM)] * len(arrays),
        out_specs=[pl.BlockSpec(memory_space=pl.ANY)] * len(arrays),
        scratch_shapes=[pltpu.SemaphoreType.DMA((len(arrays),))],
        name="deliver",
    )(*arrays)


def per_device(
    latents,
    cotangent,
    gn_gain,
    gn_bias,
    conv_weight,
    master,
    moment_one,
    moment_two,
    departing,
    partner,
):
    results = exchange(
        latents.reshape(PIX, -1),
        cotangent.reshape(PIX, -1),
        gn_gain,
        gn_bias,
        conv_weight,
        master,
        moment_one,
        moment_two,
        departing,
        partner,
    )
    forward, *states = deliver(*results)
    states = [jnp.transpose(state, (1, 0, 2))[None] for state in states]
    return (forward.reshape(cotangent.shape), *states)


def solution(mesh):
    return jax.shard_map(
        per_device,
        mesh=mesh,
        in_specs=(
            P(("rep", "shard"), None, None, None),
            P(("rep", "shard"), None, None, None),
            P(),
            P(),
            P("shard", None),
            P("rep", "shard"),
            P("rep", "shard"),
            P("rep", "shard"),
            P(),
            P(),
        ),
        out_specs=(
            P(("rep", "shard"), None, None, None),
            P("rep", None, None, "shard"),
            P("rep", None, None, "shard"),
            P("rep", None, None, "shard"),
        ),
        check_vma=False,
    )
```

```python
import jax
import jax.numpy as jnp
from jax import lax
from jax.experimental import pallas as pl
from jax.experimental.pallas import tpu as pltpu
from jax.sharding import PartitionSpec as P

GROUPS = 32
WIDTH = 20
MESH = pl.DeviceIdType.MESH
F32 = jnp.float32
BF16 = jnp.bfloat16
EXACT = lax.Precision.HIGHEST

beta_one = 0.9
beta_two = 0.999
step_count = 100.0
learn_rate = 0.01
weight_decay = 0.01
adam_eps = 1e-08
norm_eps = 1e-05

PIX = 1024
ROWS = 720
COLS = 20
CH = 144
NCH = 5
TM = 480
PR = 96
LAG = 2
GR = 24
ORDER_P = (2, 1, 3, 0)
ORDER_Q = (2, 3, 1, 0)


def adam(master, first_moment, second_moment, gradient):
    first_moment = beta_one * first_moment + (1.0 - beta_one) * gradient
    second_moment = beta_two * second_moment + (1.0 - beta_two) * gradient * gradient
    first_hat = first_moment / (1.0 - beta_one**step_count)
    second_hat = second_moment / (1.0 - beta_two**step_count)
    master = master - learn_rate * (
        first_hat / (jnp.sqrt(second_hat) + adam_eps) + weight_decay * master
    )
    return (master, first_moment, second_moment)


def group_totals(values, image_count, group_width):
    return jnp.sum(values, axis=(1, 2)).reshape(image_count, GROUPS, group_width).sum(-1)


def mod4(v):
    return lax.rem(v, 4)


def device(x, y, z, c):
    return ((mod4(z) * 4 + x) * 2 + c, y * 2 + lax.div(z, 4))


def piece_row(h, xq, y, zh):
    k = 4 * h + xq
    return pl.multiple_of(ROWS * (2 * y + zh) + PR * k - 48 * lax.div(k, 7), 16)


def exchange_kernel(
    x_ref, cot_ref, gain_ref, bias_ref, w_ref, ma_ref, m1_ref, m2_ref, dep_ref, par_ref,
    OUT, NMA, NM1, NM2,
    ACT, ACT_T, COT, W, WG, ACC, RX, R1R, R1L, R2R, R2L, S1R, S1L, S2R, S2L, D, Z,
    SF, COL, SB, RB, GA, SEL, SG, RG, PLACE,
    x_s, x_r, t_s, t_r, h_s, h_r, z_s, z_r, g_s, g_r, y_s, y_r, c_s, c_r, l_s,
):
    r = lax.axis_index("rep")
    s = lax.axis_index("shard")
    c = lax.rem(r, 2)
    x = mod4(lax.div(r, 2))
    zl = lax.div(r, 8)
    zh = lax.rem(s, 2)
    y = lax.div(s, 2)
    z = zh * 4 + zl
    p = x + c * (y - x)
    q = y + c * (x - y)
    sib = device(x, y, z, 1 - c)
    xpeer = [device(mod4(x + d), y, z, c) for d in range(4)]
    ypeer = [device(x, mod4(y + d), z, c) for d in range(4)]
    r1 = device(mod4(x + 1 - c), mod4(y + c), z, c)
    l1 = device(mod4(x + 3 * (1 - c)), mod4(y + 3 * c), z, c)
    r2 = device(mod4(x + c), mod4(y + 1 - c), z, c)
    l2 = device(mod4(x + 3 * c), mod4(y + 3 * (1 - c)), z, c)
    zpeer = [device(x, y, lax.rem(z + d, 8), c) for d in range(8)]
    lpeer = [device(x, y, zh * 4 + mod4(zl + d), c) for d in range(4)]
    sends = []

    def send(src, dst, ssem, rsem, dev):
        copy = pltpu.make_async_remote_copy(
            src_ref=src, dst_ref=dst, send_sem=ssem, recv_sem=rsem, device_id=dev, device_id_type=MESH
        )
        copy.start()
        return copy

    def post(*args):
        sends.append(send(*args))

    def arrived(dst, rsem):
        pltpu.make_async_remote_copy(
            src_ref=dst, dst_ref=dst, send_sem=l_s.at[0], recv_sem=rsem, device_id=sib, device_id_type=MESH
        ).wait_recv()

    def sent(src, ssem):
        pltpu.make_async_remote_copy(
            src_ref=src, dst_ref=src, send_sem=ssem, recv_sem=x_r.at[0], device_id=sib, device_id_type=MESH
        ).wait_send()

    own = pltpu.make_async_copy(w_ref, W.at[pl.ds(pl.multiple_of(ROWS * s, 16), ROWS)], l_s.at[0])
    own.start()
    cots = pltpu.make_async_copy(cot_ref, COT.at[pl.ds(32, PIX)], l_s.at[1])
    cots.start()
    barrier = pltpu.get_barrier_semaphore()
    peers = [sib] + xpeer[1:] + ypeer[1:] + zpeer[1:]
    for peer in peers:
        pl.semaphore_signal(barrier, inc=1, device_id=peer, device_id_type=MESH)
    staying = (1 - dep_ref[r]).astype(F32)

    SF[...] = jnp.zeros_like(SF)
    for n, ref in enumerate((ma_ref, m1_ref, m2_ref)):
        SF[GR * n : GR * n + COLS, :] = ref[...]
    COL[c, zl] = SF[...].astype(BF16)

    chan = lax.broadcasted_iota(jnp.int32, (640, 128), 0)
    low = lax.broadcasted_iota(jnp.int32, (640, 128), 1) * WIDTH
    member = ((chan >= low) & (chan < low + WIDTH)).astype(F32)
    chan = lax.broadcasted_iota(jnp.int32, (128, 640), 1)
    low = lax.broadcasted_iota(jnp.int32, (128, 640), 0) * WIDTH
    spread = ((chan >= low) & (chan < low + WIDTH)).astype(F32)

    def group_mean(sums):
        sums = jnp.broadcast_to(jnp.sum(sums, axis=0, keepdims=True), (8, 640))
        sums = jnp.dot(sums, member, preferred_element_type=F32, precision=EXACT)
        sums = jnp.dot(sums, spread, preferred_element_type=F32, precision=EXACT)
        return sums[0:1] * (1.0 / (PIX * WIDTH))

    def tile_of(i):
        return x_ref[pl.ds(pl.multiple_of(i * 64, 64), 64), :].astype(F32)

    def add_tile(i, sums):
        return sums + jnp.sum(tile_of(i).reshape(8, 8, 640), axis=0)

    mean = group_mean(lax.fori_loop(0, PIX // 64, add_tile, jnp.zeros((8, 640), F32)))

    def add_square(i, sums):
        centred = tile_of(i) - mean
        return sums + jnp.sum((centred * centred).reshape(8, 8, 640), axis=0)

    variance = group_mean(lax.fori_loop(0, PIX // 64, add_square, jnp.zeros((8, 640), F32)))
    bias = bias_ref[...].reshape(1, 640)
    scale = lax.rsqrt(variance + norm_eps) * gain_ref[...].reshape(1, 640)

    own.wait()
    pl.semaphore_wait(barrier, len(peers))

    def gather_z(buf, ss, rs, steps=(2, 3, 1)):
        for d in steps:
            post(buf.at[c, zl], buf.at[c, zl], ss.at[d - 1], rs.at[d - 1], lpeer[d])

    def gather_pair(buf, ss, rs):
        for d in (2, 3, 1):
            arrived(buf.at[c, mod4(zl + 4 - d)], rs.at[d - 1])
        post(buf.at[c], buf.at[c], ss.at[3], rs.at[3], sib)

    def rep_at(d):
        return (zl * 4 + mod4(x + d)) * 2 + c

    def states_select():
        arrived(COL.at[1 - c], t_r.at[3])
        for d in range(4):
            mate = par_ref[rep_at(d)]
            block = COL[lax.rem(mate, 2), lax.div(mate, 8)]
            if d == 0:
                RB[0] = block
            else:
                SB[d - 1] = block
                post(SB.at[d - 1], RB.at[d], t_s.at[3 + d], t_r.at[3 + d], xpeer[d])

    def columns_prepare():
        slot = lax.broadcasted_iota(jnp.int32, (48, 640), 0)
        col = lax.broadcasted_iota(jnp.int32, (48, 640), 1)
        for d in range(4):
            rep = rep_at(d)
            base = jnp.where(slot < GR, rep * COLS, par_ref[rep] * COLS - GR) + slot
            SEL[48 * d : 48 * (d + 1), :] = (col == base).astype(F32).astype(BF16)
        row = lax.broadcasted_iota(jnp.int32, (2 * PR, ROWS), 0)
        col = lax.broadcasted_iota(jnp.int32, (2 * PR, ROWS), 1)
        for d in range(4):
            xs = mod4(x + 4 - d)
            dup = 48 * lax.div(xs, 3)
            base = row + PR * xs + jnp.where(row < PR, 0, 3 * PR - dup)
            keep = (row < PR) | (row >= PR + dup)
            PLACE[d] = ((col == base) & keep).astype(F32).astype(BF16)

    def columns_select():
        arrived(GA.at[1 - c], h_r.at[3])
        rows = GA[...].astype(F32).reshape(2 * PR, 640).astype(BF16)
        picked = lax.dot_general(
            SEL[...], rows, (((1,), (1,)), ((), ())), preferred_element_type=F32
        ).astype(BF16)
        RG[0] = picked[0:48]
        for d in range(1, 4):
            SG[d - 1] = picked[48 * d : 48 * (d + 1)]
            post(SG.at[d - 1], RG.at[d], h_s.at[3 + d], h_r.at[3 + d], xpeer[d])

    def optimize():
        picked = jnp.dot(RG[0], PLACE[0], preferred_element_type=F32)
        for d in (1, 3, 2):
            arrived(RG.at[d], h_r.at[3 + d])
            arrived(RB.at[d], t_r.at[3 + d])
            picked = picked + jnp.dot(RG[d], PLACE[d], preferred_element_type=F32)
        picked = picked * (1.0 / 128.0)
        mate = par_ref[r]
        block = RB[lax.rem(x + 4 - mod4(lax.div(mate, 2)), 4)].astype(F32)
        held = [ref[...] for ref in (ma_ref, m1_ref, m2_ref)]
        mates = [block[GR * n : GR * n + COLS] for n in range(3)]
        for n, state, grad in ((0, held, picked[0:COLS]), (1, mates, picked[GR : GR + COLS])):
            for ref, value in zip((NMA, NM1, NM2), adam(*state, grad)):
                ref[:, n, :] = value * staying

    up = mod4(y + 3 - 2 * c)
    far = mod4(y + 2)
    ynd = device(x, mod4(y + 1 + 2 * c), z, c)
    znd = device(x, y, lax.rem(z + 1 + 6 * c, 8), c)

    def wchunk(yy, hh, k):
        return W.at[pl.ds(pl.multiple_of(ROWS * (2 * yy + hh) + CH * k, 16), CH)]

    pos = (1 - c) * zl + c * (3 - zl)
    last = lax.div(pos, 3)

    def entry(n, cc):
        v = n + 3 * cc + 2 * lax.div(n + 7 - 4 * cc, 10)
        t = lax.div(v, 5)
        return mod4(y + 8 + t * (3 - 2 * cc) + lax.div(t * (t - 1), 2) * (4 * cc - 4)), lax.rem(v, 5)

    def z_send(n):
        m, k = entry(n, c)
        send(wchunk(m, zh, k), wchunk(m, zh, k), z_s.at[8 + n], z_r.at[8 + n], znd)

    def weights_start():
        for k in range(NCH):
            post(wchunk(y, zh, k), wchunk(y, zh, k), y_s.at[k], y_r.at[k], ynd)

        @pl.when(last == 1)
        def _():
            z_send(0)
            z_send(1)

        @pl.when((last == 1) & (c == 0))
        def _():
            z_send(2)

    def weights_y(k):
        chunk = wchunk(up, zh, k)
        arrived(chunk, y_r.at[k])

        @pl.when(c == (0 if k < 2 else 1))
        def _():
            send(chunk, chunk, y_s.at[NCH + k], y_r.at[NCH + k], ynd)

        @pl.when(last == 1)
        def _():
            z_send(3 + k - c)

        post(chunk, chunk, c_s.at[k], c_r.at[k], sib)

    def weights_far():
        for k in range(NCH):

            @pl.when(c == (0 if k < 2 else 1))
            def _():
                chunk = wchunk(far, zh, k)
                arrived(chunk, y_r.at[NCH + k])
                send(chunk, chunk, c_s.at[NCH + k], c_r.at[NCH + k], sib)

        @pl.when(last == 1)
        def _():
            z_send(8)
            z_send(9)

        @pl.when((last == 1) & (c == 1))
        def _():
            z_send(7)

    def weights_z(slot):
        n = slot - LAG * pos

        @pl.when((n >= 0) & (n < 10))
        def _():
            m, k = entry(n, c)
            chunk = wchunk(m, 1 - zh, k)
            arrived(chunk, z_r.at[8 + n])

            @pl.when(last == 0)
            def _():
                send(chunk, chunk, z_s.at[8 + n], z_r.at[8 + n], znd)

            send(chunk, chunk, c_s.at[10 + n], c_r.at[10 + n], sib)

    def weights_wait():
        cs = 1 - c
        for k in range(NCH):
            arrived(wchunk(mod4(y + 3 - 2 * cs), zh, k), c_r.at[k])

            @pl.when(c == (1 if k < 2 else 0))
            def _():
                arrived(wchunk(far, zh, k), c_r.at[NCH + k])

        for n in range(10):
            m, k = entry(n, cs)
            arrived(wchunk(m, 1 - zh, k), c_r.at[10 + n])

    def weights_sent():
        for n in range(10):
            sent(wchunk(0, 0, 0), z_s.at[8 + n])
            sent(wchunk(0, 0, 0), c_s.at[10 + n])
        for k in range(NCH):

            @pl.when(c == (0 if k < 2 else 1))
            def _():
                sent(wchunk(0, 0, 0), y_s.at[NCH + k])
                sent(wchunk(0, 0, 0), c_s.at[NCH + k])

    def terms(i, lo=0, hi=3):
        yy = mod4(y + ORDER_Q[i])

        def tile(k, carry):
            m = yy * 3 + k
            tap_row = lax.div(m, 4)
            lhs = ACT_T[pl.ds(pl.multiple_of(TM * mod4(m), 16), TM), :]
            rhs = COT[pl.ds(pl.multiple_of(32 * (2 - tap_row), 32), PIX), :]
            product = jnp.dot(lhs, rhs, preferred_element_type=F32)
            WG[pl.ds(pl.multiple_of(TM * m, 16), TM), :] = (product * staying).astype(BF16)
            return carry

        lax.fori_loop(lo, hi, tile, 0)

    def pair_send(i):
        cs = 1 - c
        yy = mod4(y + ORDER_Q[i])
        for xq in range(4):
            a, b = xq + cs * (yy - xq), yy + cs * (xq - yy)
            for zz in range(2):
                n = (xq * 4 + yy) * 2 + zz
                post(WG.at[pl.ds(piece_row(cs, xq, yy, zz), PR)], RX.at[a, b, zz], x_s.at[n], x_r.at[n], sib)

    def chip_sum(di, oi, zz, extra=(), into=None):
        a, b = mod4(p + ORDER_P[di]), mod4(q + ORDER_Q[oi])
        xq, yy = a + c * (b - a), b + c * (a - b)
        row = piece_row(c, xq, yy, zz)
        arrived(RX.at[a, b, zz], x_r.at[(xq * 4 + yy) * 2 + zz])
        if into is None:

            def body(i, carry):
                k = pl.multiple_of(i * 16, 16)
                total = RX[a, b, zz, pl.ds(k, 16), :].astype(F32) + WG[pl.ds(row + k, 16), :].astype(F32)
                for ref in extra:
                    total = total + ref[pl.ds(k, 16), :].astype(F32)
                RX[a, b, zz, pl.ds(k, 16), :] = total.astype(BF16)
                return carry

            lax.fori_loop(0, PR // 16, body, 0)
        else:
            total = RX[a, b, zz].astype(F32) + WG[pl.ds(row, PR), :].astype(F32)
            for ref in extra:
                total = total + ref[...].astype(F32)
            for g in range(4):
                into[zz, g] = total[GR * g : GR * (g + 1)].astype(BF16)
        return a, b

    def conv(a):
        def tile(i, carry):
            at = pl.ds(pl.multiple_of(256 * i, 256), 256)
            lhs = ACT[pl.ds(pl.multiple_of(256 * i + 32 * a, 32), 256), :]
            total = jnp.dot(lhs, W[1920 * a : 1920 * (a + 1), :], preferred_element_type=F32)
            if a > 0:
                total = total + ACC[at, :]
            if a < 2:
                ACC[at, :] = total
            else:
                OUT[at, :] = total.astype(BF16)
            return carry

        lax.fori_loop(0, 4, tile, 0)

    weights_start()
    gather_z(COL, t_s, t_r)

    edge = jnp.zeros((32, 1920), BF16)
    ACT[0:32, :] = edge
    ACT[PIX + 32 : PIX + 64, :] = edge
    COT[0:32, :] = edge[:, 0:640]
    COT[PIX + 32 : PIX + 64, :] = edge[:, 0:640]

    def activate(i, carry):
        value = x_ref[pl.ds(pl.multiple_of(i * 128, 128), 128), :].astype(F32)
        value = (value - mean) * scale + bias
        value = value * (0.5 * jnp.tanh(0.5 * value) + 0.5)
        column = lax.broadcasted_iota(jnp.int32, (128, 640), 0) & 31
        for b in range(3):
            if b == 0:
                part = jnp.where(column == 0, 0.0, pltpu.roll(value, 1, 0))
            elif b == 1:
                part = value
            else:
                part = jnp.where(column == 31, 0.0, pltpu.roll(value, 127, 0))
            ACT[pl.ds(pl.multiple_of(i * 128 + 32, 32), 128), 640 * b : 640 * (b + 1)] = part.astype(BF16)
            ACT_T[640 * b : 640 * (b + 1), pl.ds(pl.multiple_of(i * 128, 128), 128)] = part.T.astype(BF16)
        return carry

    lax.fori_loop(0, PIX // 128, activate, 0)
    cots.wait()
    def first_step(oi):
        a, b = chip_sum(0, oi, 0)
        post(RX.at[a, b, 0], R1R.at[oi], g_s.at[oi], g_r.at[oi], r1)
        chip_sum(0, oi, 1)
        post(RX.at[a, b, 1], R1L.at[oi], g_s.at[4 + oi], g_r.at[4 + oi], l1)

    def second_step(oi):
        arrived(R1R.at[oi], g_r.at[oi])
        a, b = chip_sum(1, oi, 0, (R1R.at[oi],))
        chip_sum(1, oi, 1)
        post(RX.at[a, b], R2R.at[oi], g_s.at[8 + oi], g_r.at[8 + oi], r1)
        arrived(R1L.at[oi], g_r.at[4 + oi])
        chip_sum(2, oi, 0)
        a, b = chip_sum(2, oi, 1, (R1L.at[oi],))
        post(RX.at[a, b], R2L.at[oi], g_s.at[12 + oi], g_r.at[12 + oi], l1)

    terms(0)
    pair_send(0)
    weights_y(0)
    weights_y(1)
    weights_z(0)
    terms(1, 0, 2)
    weights_z(1)
    terms(1, 2, 3)
    pair_send(1)
    first_step(0)
    weights_y(2)
    weights_y(3)
    weights_z(2)
    terms(2, 0, 2)
    weights_y(4)
    weights_z(3)
    terms(2, 2, 3)
    pair_send(2)
    first_step(1)
    weights_z(4)
    terms(3, 0, 2)
    weights_z(5)
    terms(3, 2, 3)
    pair_send(3)
    weights_far()
    weights_z(6)
    first_step(2)
    weights_z(7)
    first_step(3)
    weights_z(8)
    second_step(0)
    weights_z(9)
    gather_pair(COL, t_s, t_r)
    columns_prepare()
    second_step(1)
    weights_z(10)
    second_step(2)
    weights_z(11)
    second_step(3)
    weights_z(12)
    for oi in range(4):
        arrived(R2R.at[oi], g_r.at[8 + oi])
        arrived(R2L.at[oi], g_r.at[12 + oi])
        extra = [[R2R.at[oi, zz], R2L.at[oi, zz]] for zz in range(2)]
        if oi == 1:
            arrived(S1L, g_r.at[17])
            extra[1].append(S1L)
        if oi == 2:
            arrived(S1R, g_r.at[16])
            extra[0].append(S1R)
        if oi == 3:
            arrived(S2R, g_r.at[18])
            arrived(S2L, g_r.at[19])
            extra[0] += [S2R.at[0], S2L.at[0]]
            extra[1] += [S2R.at[1], S2L.at[1]]
        for zz in range(2):
            a, b = chip_sum(3, oi, zz, extra[zz], D if oi == 3 else None)
        if oi == 0:
            post(RX.at[a, b, 0], S1R, g_s.at[16], g_r.at[16], r2)
            post(RX.at[a, b, 1], S1L, g_s.at[17], g_r.at[17], l2)
        if oi == 1:
            post(RX.at[a, b], S2L, g_s.at[19], g_r.at[19], l2)
        if oi == 2:
            post(RX.at[a, b], S2R, g_s.at[18], g_r.at[18], r2)
        if oi < 3:
            weights_z(13 + oi)
    for d in (4, 3, 5, 2, 6, 1, 7):
        zz = lax.rem(z + d, 8)
        post(D.at[lax.div(zz, 4), mod4(zz)], Z.at[d], z_s.at[d], z_r.at[d], zpeer[d])
    weights_wait()
    conv(0)
    states_select()
    total = D[zh, zl].astype(F32)
    for d in (1, 7, 2, 6, 3, 5, 4):
        arrived(Z.at[d], z_r.at[d])
        total = total + Z[d].astype(F32)
    GA[c, zl] = total.astype(BF16)
    gather_z(GA, h_s, h_r)
    conv(1)
    gather_pair(GA, h_s, h_r)
    columns_select()
    conv(2)
    optimize()
    weights_sent()
    for copy in sends:
        copy.wait_send()


def exchange(latents, cotangent, gain, bias, weight, master, moment_one, moment_two, departing, partner):
    dma = pltpu.SemaphoreType.DMA
    vmem, smem = pl.BlockSpec(memory_space=pltpu.VMEM), pl.BlockSpec(memory_space=pltpu.SMEM)
    anywhere = pl.BlockSpec(memory_space=pl.ANY)
    half = pltpu.VMEM((PR, 640), BF16)
    state = jax.ShapeDtypeStruct((COLS, 2, ROWS), F32)
    return pl.pallas_call(
        exchange_kernel,
        out_shape=(jax.ShapeDtypeStruct((PIX, 640), BF16), state, state, state),
        in_specs=[vmem, anywhere, vmem, vmem, anywhere, vmem, vmem, vmem, smem, smem],
        out_specs=[vmem] * 4,
        scratch_shapes=[
            pltpu.VMEM((PIX + 64, 1920), BF16),
            pltpu.VMEM((1920, PIX), BF16),
            pltpu.VMEM((PIX + 64, 640), BF16),
            pltpu.VMEM((8 * ROWS, 640), BF16),
            pltpu.VMEM((8 * ROWS, 640), BF16),
            pltpu.VMEM((PIX, 640), F32),
            pltpu.VMEM((4, 4, 2, PR, 640), BF16),
            pltpu.VMEM((4, PR, 640), BF16),
            pltpu.VMEM((4, PR, 640), BF16),
            pltpu.VMEM((4, 2, PR, 640), BF16),
            pltpu.VMEM((4, 2, PR, 640), BF16),
            half,
            half,
            pltpu.VMEM((2, PR, 640), BF16),
            pltpu.VMEM((2, PR, 640), BF16),
            pltpu.VMEM((2, 4, GR, 640), BF16),
            pltpu.VMEM((8, GR, 640), BF16),
            pltpu.VMEM((3 * GR, ROWS), F32),
            pltpu.VMEM((2, 4, 3 * GR, ROWS), BF16),
            pltpu.VMEM((3, 3 * GR, ROWS), BF16),
            pltpu.VMEM((4, 3 * GR, ROWS), BF16),
            pltpu.VMEM((2, 4, GR, 640), BF16),
            pltpu.VMEM((4 * 48, 640), BF16),
            pltpu.VMEM((3, 48, 2 * PR), BF16),
            pltpu.VMEM((4, 48, 2 * PR), BF16),
            pltpu.VMEM((4, 2 * PR, ROWS), BF16),
            dma((32,)), dma((32,)),
            dma((7,)), dma((7,)),
            dma((7,)), dma((7,)),
            dma((18,)), dma((18,)),
            dma((20,)), dma((20,)),
            dma((10,)), dma((10,)),
            dma((20,)), dma((20,)),
            dma((2,)),
        ],
        compiler_params=pltpu.CompilerParams(
            collective_id=0, has_side_effects=True, vmem_limit_bytes=60 * 1024 * 1024
        ),
        name="exchange",
    )(latents, cotangent, gain, bias, weight, master, moment_one, moment_two, departing, partner)


def deliver_kernel(*refs):
    count = len(refs) // 2
    copies = [
        pltpu.make_async_copy(refs[n], refs[count + n], refs[-1].at[n]) for n in range(count)
    ]
    for copy in copies:
        copy.start()
    for copy in copies:
        copy.wait()


def deliver(*arrays):
    return pl.pallas_call(
        deliver_kernel,
        out_shape=tuple(jax.ShapeDtypeStruct(v.shape, v.dtype) for v in arrays),
        in_specs=[pl.BlockSpec(memory_space=pltpu.VMEM)] * len(arrays),
        out_specs=[pl.BlockSpec(memory_space=pl.ANY)] * len(arrays),
        scratch_shapes=[pltpu.SemaphoreType.DMA((len(arrays),))],
        name="deliver",
    )(*arrays)


def per_device(
    latents,
    cotangent,
    gn_gain,
    gn_bias,
    conv_weight,
    master,
    moment_one,
    moment_two,
    departing,
    partner,
):
    results = exchange(
        latents.reshape(PIX, -1),
        cotangent.reshape(PIX, -1),
        gn_gain,
        gn_bias,
        conv_weight,
        master,
        moment_one,
        moment_two,
        departing,
        partner,
    )
    forward, *states = deliver(*results)
    states = [jnp.transpose(state, (1, 0, 2))[None] for state in states]
    return (forward.reshape(cotangent.shape), *states)


def solution(mesh):
    return jax.shard_map(
        per_device,
        mesh=mesh,
        in_specs=(
            P(("rep", "shard"), None, None, None),
            P(("rep", "shard"), None, None, None),
            P(),
            P(),
            P("shard", None),
            P("rep", "shard"),
            P("rep", "shard"),
            P("rep", "shard"),
            P(),
            P(),
        ),
        out_specs=(
            P(("rep", "shard"), None, None, None),
            P("rep", None, None, "shard"),
            P("rep", None, None, "shard"),
            P("rep", None, None, "shard"),
        ),
        check_vma=False,
    )
```

```python
import jax
import jax.numpy as jnp
from jax import lax
from jax.experimental import pallas as pl
from jax.experimental.pallas import tpu as pltpu
from jax.sharding import PartitionSpec as P

GROUPS = 32
WIDTH = 20
MESH = pl.DeviceIdType.MESH
F32 = jnp.float32
BF16 = jnp.bfloat16
EXACT = lax.Precision.HIGHEST

beta_one = 0.9
beta_two = 0.999
step_count = 100.0
learn_rate = 0.01
weight_decay = 0.01
adam_eps = 1e-08
norm_eps = 1e-05

PIX = 1024
ROWS = 720
COLS = 20
CH = 144
NCH = 5
TM = 480
PR = 96
LAG = 2
GR = 24
ORDER_P = (2, 1, 3, 0)
ORDER_Q = (2, 3, 1, 0)


def adam(master, first_moment, second_moment, gradient):
    first_moment = beta_one * first_moment + (1.0 - beta_one) * gradient
    second_moment = beta_two * second_moment + (1.0 - beta_two) * gradient * gradient
    first_hat = first_moment / (1.0 - beta_one**step_count)
    second_hat = second_moment / (1.0 - beta_two**step_count)
    master = master - learn_rate * (
        first_hat / (jnp.sqrt(second_hat) + adam_eps) + weight_decay * master
    )
    return (master, first_moment, second_moment)


def group_totals(values, image_count, group_width):
    return jnp.sum(values, axis=(1, 2)).reshape(image_count, GROUPS, group_width).sum(-1)


def mod4(v):
    return lax.rem(v, 4)


def device(x, y, z, c):
    return ((mod4(z) * 4 + x) * 2 + c, y * 2 + lax.div(z, 4))


def piece_row(h, xq, y, zh):
    k = 4 * h + xq
    return pl.multiple_of(ROWS * (2 * y + zh) + PR * k - 48 * lax.div(k, 7), 16)


def exchange_kernel(
    x_ref, cot_ref, gain_ref, bias_ref, w_ref, ma_ref, m1_ref, m2_ref, dep_ref, par_ref,
    OUT, NMA, NM1, NM2,
    ACT, ACT_T, COT, W, WG, ACC, RX, R1R, R1L, R2R, R2L, S1R, S1L, S2R, S2L, D, Z,
    SF, COL, SB, RB, GA, SEL, SG, RG, PLACE,
    x_s, x_r, t_s, t_r, h_s, h_r, z_s, z_r, g_s, g_r, y_s, y_r, c_s, c_r, l_s,
):
    r = lax.axis_index("rep")
    s = lax.axis_index("shard")
    c = lax.rem(r, 2)
    x = mod4(lax.div(r, 2))
    zl = lax.div(r, 8)
    zh = lax.rem(s, 2)
    y = lax.div(s, 2)
    z = zh * 4 + zl
    p = x + c * (y - x)
    q = y + c * (x - y)
    sib = device(x, y, z, 1 - c)
    xpeer = [device(mod4(x + d), y, z, c) for d in range(4)]
    ypeer = [device(x, mod4(y + d), z, c) for d in range(4)]
    r1 = device(mod4(x + 1 - c), mod4(y + c), z, c)
    l1 = device(mod4(x + 3 * (1 - c)), mod4(y + 3 * c), z, c)
    r2 = device(mod4(x + c), mod4(y + 1 - c), z, c)
    l2 = device(mod4(x + 3 * c), mod4(y + 3 * (1 - c)), z, c)
    zpeer = [device(x, y, lax.rem(z + d, 8), c) for d in range(8)]
    lpeer = [device(x, y, zh * 4 + mod4(zl + d), c) for d in range(4)]
    sends = []

    def send(src, dst, ssem, rsem, dev):
        copy = pltpu.make_async_remote_copy(
            src_ref=src, dst_ref=dst, send_sem=ssem, recv_sem=rsem, device_id=dev, device_id_type=MESH
        )
        copy.start()
        return copy

    def post(*args):
        sends.append(send(*args))

    def arrived(dst, rsem):
        pltpu.make_async_remote_copy(
            src_ref=dst, dst_ref=dst, send_sem=l_s.at[0], recv_sem=rsem, device_id=sib, device_id_type=MESH
        ).wait_recv()

    def sent(src, ssem):
        pltpu.make_async_remote_copy(
            src_ref=src, dst_ref=src, send_sem=ssem, recv_sem=x_r.at[0], device_id=sib, device_id_type=MESH
        ).wait_send()

    own = pltpu.make_async_copy(w_ref, W.at[pl.ds(pl.multiple_of(ROWS * s, 16), ROWS)], l_s.at[0])
    own.start()
    cots = pltpu.make_async_copy(cot_ref, COT.at[pl.ds(32, PIX)], l_s.at[1])
    cots.start()
    barrier = pltpu.get_barrier_semaphore()
    peers = [sib] + xpeer[1:] + ypeer[1:] + zpeer[1:]
    for peer in peers:
        pl.semaphore_signal(barrier, inc=1, device_id=peer, device_id_type=MESH)
    staying = (1 - dep_ref[r]).astype(F32)

    SF[...] = jnp.zeros_like(SF)
    for n, ref in enumerate((ma_ref, m1_ref, m2_ref)):
        SF[GR * n : GR * n + COLS, :] = ref[...]
    COL[c, zl] = SF[...].astype(BF16)

    chan = lax.broadcasted_iota(jnp.int32, (640, 128), 0)
    low = lax.broadcasted_iota(jnp.int32, (640, 128), 1) * WIDTH
    member = ((chan >= low) & (chan < low + WIDTH)).astype(F32)
    chan = lax.broadcasted_iota(jnp.int32, (128, 640), 1)
    low = lax.broadcasted_iota(jnp.int32, (128, 640), 0) * WIDTH
    spread = ((chan >= low) & (chan < low + WIDTH)).astype(F32)

    def group_mean(sums):
        sums = jnp.broadcast_to(jnp.sum(sums, axis=0, keepdims=True), (8, 640))
        sums = jnp.dot(sums, member, preferred_element_type=F32, precision=EXACT)
        sums = jnp.dot(sums, spread, preferred_element_type=F32, precision=EXACT)
        return sums[0:1] * (1.0 / (PIX * WIDTH))

    def tile_of(i):
        return x_ref[pl.ds(pl.multiple_of(i * 64, 64), 64), :].astype(F32)

    def add_tile(i, sums):
        return sums + jnp.sum(tile_of(i).reshape(8, 8, 640), axis=0)

    mean = group_mean(lax.fori_loop(0, PIX // 64, add_tile, jnp.zeros((8, 640), F32)))

    def add_square(i, sums):
        centred = tile_of(i) - mean
        return sums + jnp.sum((centred * centred).reshape(8, 8, 640), axis=0)

    variance = group_mean(lax.fori_loop(0, PIX // 64, add_square, jnp.zeros((8, 640), F32)))
    bias = bias_ref[...].reshape(1, 640)
    scale = lax.rsqrt(variance + norm_eps) * gain_ref[...].reshape(1, 640)

    own.wait()
    pl.semaphore_wait(barrier, len(peers))

    def gather_z(buf, ss, rs, steps=(2, 3, 1)):
        for d in steps:
            post(buf.at[c, zl], buf.at[c, zl], ss.at[d - 1], rs.at[d - 1], lpeer[d])

    def gather_pair(buf, ss, rs):
        for d in (2, 3, 1):
            arrived(buf.at[c, mod4(zl + 4 - d)], rs.at[d - 1])
        post(buf.at[c], buf.at[c], ss.at[3], rs.at[3], sib)

    def rep_at(d):
        return (zl * 4 + mod4(x + d)) * 2 + c

    def states_select():
        arrived(COL.at[1 - c], t_r.at[3])
        for d in range(4):
            mate = par_ref[rep_at(d)]
            block = COL[lax.rem(mate, 2), lax.div(mate, 8)]
            if d == 0:
                RB[0] = block
            else:
                SB[d - 1] = block
                post(SB.at[d - 1], RB.at[d], t_s.at[3 + d], t_r.at[3 + d], xpeer[d])

    def columns_prepare():
        slot = lax.broadcasted_iota(jnp.int32, (48, 640), 0)
        col = lax.broadcasted_iota(jnp.int32, (48, 640), 1)
        for d in range(4):
            rep = rep_at(d)
            base = jnp.where(slot < GR, rep * COLS, par_ref[rep] * COLS - GR) + slot
            SEL[48 * d : 48 * (d + 1), :] = (col == base).astype(F32).astype(BF16)
        row = lax.broadcasted_iota(jnp.int32, (2 * PR, ROWS), 0)
        col = lax.broadcasted_iota(jnp.int32, (2 * PR, ROWS), 1)
        for d in range(4):
            xs = mod4(x + 4 - d)
            dup = 48 * lax.div(xs, 3)
            base = row + PR * xs + jnp.where(row < PR, 0, 3 * PR - dup)
            keep = (row < PR) | (row >= PR + dup)
            PLACE[d] = ((col == base) & keep).astype(F32).astype(BF16)

    def columns_select():
        arrived(GA.at[1 - c], h_r.at[3])
        rows = GA[...].astype(F32).reshape(2 * PR, 640).astype(BF16)
        picked = lax.dot_general(
            SEL[...], rows, (((1,), (1,)), ((), ())), preferred_element_type=F32
        ).astype(BF16)
        RG[0] = picked[0:48]
        for d in range(1, 4):
            SG[d - 1] = picked[48 * d : 48 * (d + 1)]
            post(SG.at[d - 1], RG.at[d], h_s.at[3 + d], h_r.at[3 + d], xpeer[d])

    def optimize():
        picked = jnp.dot(RG[0], PLACE[0], preferred_element_type=F32)
        for d in (1, 3, 2):
            arrived(RG.at[d], h_r.at[3 + d])
            arrived(RB.at[d], t_r.at[3 + d])
            picked = picked + jnp.dot(RG[d], PLACE[d], preferred_element_type=F32)
        picked = picked * (1.0 / 128.0)
        mate = par_ref[r]
        block = RB[lax.rem(x + 4 - mod4(lax.div(mate, 2)), 4)].astype(F32)
        held = [ref[...] for ref in (ma_ref, m1_ref, m2_ref)]
        mates = [block[GR * n : GR * n + COLS] for n in range(3)]
        for n, state, grad in ((0, held, picked[0:COLS]), (1, mates, picked[GR : GR + COLS])):
            for ref, value in zip((NMA, NM1, NM2), adam(*state, grad)):
                ref[:, n, :] = value * staying

    up = mod4(y + 3 - 2 * c)
    far = mod4(y + 2)
    ynd = device(x, mod4(y + 1 + 2 * c), z, c)
    znd = device(x, y, lax.rem(z + 1 + 6 * c, 8), c)

    def wchunk(yy, hh, k):
        return W.at[pl.ds(pl.multiple_of(ROWS * (2 * yy + hh) + CH * k, 16), CH)]

    pos = (1 - c) * zl + c * (3 - zl)
    last = lax.div(pos, 3)

    def entry(n, cc):
        v = n + 3 * cc + 2 * lax.div(n + 7 - 4 * cc, 10)
        t = lax.div(v, 5)
        return mod4(y + 8 + t * (3 - 2 * cc) + lax.div(t * (t - 1), 2) * (4 * cc - 4)), lax.rem(v, 5)

    def z_send(n):
        m, k = entry(n, c)
        send(wchunk(m, zh, k), wchunk(m, zh, k), z_s.at[8 + n], z_r.at[8 + n], znd)

    def weights_start():
        for k in range(NCH):
            post(wchunk(y, zh, k), wchunk(y, zh, k), y_s.at[k], y_r.at[k], ynd)

        @pl.when(last == 1)
        def _():
            z_send(0)
            z_send(1)

        @pl.when((last == 1) & (c == 0))
        def _():
            z_send(2)

    def weights_y(k):
        chunk = wchunk(up, zh, k)
        arrived(chunk, y_r.at[k])

        @pl.when(c == (0 if k < 2 else 1))
        def _():
            send(chunk, chunk, y_s.at[NCH + k], y_r.at[NCH + k], ynd)

        @pl.when(last == 1)
        def _():
            z_send(3 + k - c)

        post(chunk, chunk, c_s.at[k], c_r.at[k], sib)

    def weights_far():
        for k in range(NCH):

            @pl.when(c == (0 if k < 2 else 1))
            def _():
                chunk = wchunk(far, zh, k)
                arrived(chunk, y_r.at[NCH + k])
                send(chunk, chunk, c_s.at[NCH + k], c_r.at[NCH + k], sib)

        @pl.when(last == 1)
        def _():
            z_send(8)
            z_send(9)

        @pl.when((last == 1) & (c == 1))
        def _():
            z_send(7)

    def weights_z(slot):
        n = slot - LAG * pos

        @pl.when((n >= 0) & (n < 10))
        def _():
            m, k = entry(n, c)
            chunk = wchunk(m, 1 - zh, k)
            arrived(chunk, z_r.at[8 + n])

            @pl.when(last == 0)
            def _():
                send(chunk, chunk, z_s.at[8 + n], z_r.at[8 + n], znd)

            send(chunk, chunk, c_s.at[10 + n], c_r.at[10 + n], sib)

    def from_other(n):
        m, k = entry(n, 1 - c)
        arrived(wchunk(m, 1 - zh, k), c_r.at[10 + n])

    def weights_near():
        for k in range(NCH):
            arrived(wchunk(mod4(y + 1 + 2 * c), zh, k), c_r.at[k])
        for n in range(7):
            from_other(n)

        @pl.when(c == 1)
        def _():
            from_other(7)

    def weights_wait():
        for k in range(NCH):

            @pl.when(c == (1 if k < 2 else 0))
            def _():
                arrived(wchunk(far, zh, k), c_r.at[NCH + k])

        @pl.when(c == 0)
        def _():
            from_other(7)

        from_other(8)
        from_other(9)

    def weights_sent():
        for n in range(10):
            sent(wchunk(0, 0, 0), z_s.at[8 + n])
            sent(wchunk(0, 0, 0), c_s.at[10 + n])
        for k in range(NCH):

            @pl.when(c == (0 if k < 2 else 1))
            def _():
                sent(wchunk(0, 0, 0), y_s.at[NCH + k])
                sent(wchunk(0, 0, 0), c_s.at[NCH + k])

    def terms(i, lo=0, hi=3):
        yy = mod4(y + ORDER_Q[i])

        def tile(k, carry):
            m = yy * 3 + k
            tap_row = lax.div(m, 4)
            lhs = ACT_T[pl.ds(pl.multiple_of(TM * mod4(m), 16), TM), :]
            rhs = COT[pl.ds(pl.multiple_of(32 * (2 - tap_row), 32), PIX), :]
            product = jnp.dot(lhs, rhs, preferred_element_type=F32)
            WG[pl.ds(pl.multiple_of(TM * m, 16), TM), :] = (product * staying).astype(BF16)
            return carry

        lax.fori_loop(lo, hi, tile, 0)

    def pair_send(i):
        cs = 1 - c
        yy = mod4(y + ORDER_Q[i])
        for xq in range(4):
            a, b = xq + cs * (yy - xq), yy + cs * (xq - yy)
            for zz in range(2):
                n = (xq * 4 + yy) * 2 + zz
                post(WG.at[pl.ds(piece_row(cs, xq, yy, zz), PR)], RX.at[a, b, zz], x_s.at[n], x_r.at[n], sib)

    def chip_sum(di, oi, zz, extra=(), into=None):
        a, b = mod4(p + ORDER_P[di]), mod4(q + ORDER_Q[oi])
        xq, yy = a + c * (b - a), b + c * (a - b)
        row = piece_row(c, xq, yy, zz)
        arrived(RX.at[a, b, zz], x_r.at[(xq * 4 + yy) * 2 + zz])
        if into is None:

            def body(i, carry):
                k = pl.multiple_of(i * 16, 16)
                total = RX[a, b, zz, pl.ds(k, 16), :].astype(F32) + WG[pl.ds(row + k, 16), :].astype(F32)
                for ref in extra:
                    total = total + ref[pl.ds(k, 16), :].astype(F32)
                RX[a, b, zz, pl.ds(k, 16), :] = total.astype(BF16)
                return carry

            lax.fori_loop(0, PR // 16, body, 0)
        else:
            total = RX[a, b, zz].astype(F32) + WG[pl.ds(row, PR), :].astype(F32)
            for ref in extra:
                total = total + ref[...].astype(F32)
            for g in range(4):
                into[zz, g] = total[GR * g : GR * (g + 1)].astype(BF16)
        return a, b

    first_third = (1 + far) * (1 - lax.div(far, 2))

    def conv(turn, lo=0, hi=4):
        a = lax.rem(first_third + turn, 3)

        def tile(i, carry):
            at = pl.ds(pl.multiple_of(256 * i, 256), 256)
            lhs = ACT[pl.ds(pl.multiple_of(256 * i + 32 * a, 32), 256), :]
            total = jnp.dot(lhs, W[pl.ds(pl.multiple_of(1920 * a, 128), 1920), :], preferred_element_type=F32)
            if turn > 0:
                total = total + ACC[at, :]
            if turn < 2:
                ACC[at, :] = total
            else:
                OUT[at, :] = total.astype(BF16)
            return carry

        lax.fori_loop(lo, hi, tile, 0)

    weights_start()
    gather_z(COL, t_s, t_r)

    edge = jnp.zeros((32, 1920), BF16)
    ACT[0:32, :] = edge
    ACT[PIX + 32 : PIX + 64, :] = edge
    COT[0:32, :] = edge[:, 0:640]
    COT[PIX + 32 : PIX + 64, :] = edge[:, 0:640]

    def activate(i, carry):
        value = x_ref[pl.ds(pl.multiple_of(i * 128, 128), 128), :].astype(F32)
        value = (value - mean) * scale + bias
        value = value * (0.5 * jnp.tanh(0.5 * value) + 0.5)
        column = lax.broadcasted_iota(jnp.int32, (128, 640), 0) & 31
        for b in range(3):
            if b == 0:
                part = jnp.where(column == 0, 0.0, pltpu.roll(value, 1, 0))
            elif b == 1:
                part = value
            else:
                part = jnp.where(column == 31, 0.0, pltpu.roll(value, 127, 0))
            ACT[pl.ds(pl.multiple_of(i * 128 + 32, 32), 128), 640 * b : 640 * (b + 1)] = part.astype(BF16)
            ACT_T[640 * b : 640 * (b + 1), pl.ds(pl.multiple_of(i * 128, 128), 128)] = part.T.astype(BF16)
        return carry

    lax.fori_loop(0, PIX // 128, activate, 0)
    cots.wait()
    def first_step(oi):
        a, b = chip_sum(0, oi, 0)
        post(RX.at[a, b, 0], R1R.at[oi], g_s.at[oi], g_r.at[oi], r1)
        chip_sum(0, oi, 1)
        post(RX.at[a, b, 1], R1L.at[oi], g_s.at[4 + oi], g_r.at[4 + oi], l1)

    def second_step(oi):
        arrived(R1R.at[oi], g_r.at[oi])
        a, b = chip_sum(1, oi, 0, (R1R.at[oi],))
        chip_sum(1, oi, 1)
        post(RX.at[a, b], R2R.at[oi], g_s.at[8 + oi], g_r.at[8 + oi], r1)
        arrived(R1L.at[oi], g_r.at[4 + oi])
        chip_sum(2, oi, 0)
        a, b = chip_sum(2, oi, 1, (R1L.at[oi],))
        post(RX.at[a, b], R2L.at[oi], g_s.at[12 + oi], g_r.at[12 + oi], l1)

    terms(0)
    pair_send(0)
    weights_y(0)
    weights_y(1)
    weights_z(0)
    terms(1, 0, 2)
    weights_z(1)
    terms(1, 2, 3)
    pair_send(1)
    first_step(0)
    weights_y(2)
    weights_y(3)
    weights_z(2)
    terms(2, 0, 2)
    weights_y(4)
    weights_z(3)
    terms(2, 2, 3)
    pair_send(2)
    first_step(1)
    weights_z(4)
    terms(3, 0, 2)
    weights_z(5)
    terms(3, 2, 3)
    pair_send(3)
    weights_far()
    weights_z(6)
    first_step(2)
    weights_z(7)
    first_step(3)
    weights_z(8)
    second_step(0)
    weights_z(9)
    gather_pair(COL, t_s, t_r)
    columns_prepare()
    second_step(1)
    weights_z(10)
    second_step(2)
    weights_z(11)
    second_step(3)
    weights_z(12)
    for oi in range(4):
        arrived(R2R.at[oi], g_r.at[8 + oi])
        arrived(R2L.at[oi], g_r.at[12 + oi])
        extra = [[R2R.at[oi, zz], R2L.at[oi, zz]] for zz in range(2)]
        if oi == 1:
            arrived(S1L, g_r.at[17])
            extra[1].append(S1L)
        if oi == 2:
            arrived(S1R, g_r.at[16])
            extra[0].append(S1R)
        if oi == 3:
            arrived(S2R, g_r.at[18])
            arrived(S2L, g_r.at[19])
            extra[0] += [S2R.at[0], S2L.at[0]]
            extra[1] += [S2R.at[1], S2L.at[1]]
        for zz in range(2):
            a, b = chip_sum(3, oi, zz, extra[zz], D if oi == 3 else None)
        if oi == 0:
            post(RX.at[a, b, 0], S1R, g_s.at[16], g_r.at[16], r2)
            post(RX.at[a, b, 1], S1L, g_s.at[17], g_r.at[17], l2)
        if oi == 1:
            post(RX.at[a, b], S2L, g_s.at[19], g_r.at[19], l2)
        if oi == 2:
            post(RX.at[a, b], S2R, g_s.at[18], g_r.at[18], r2)
        if oi == 2:
            weights_z(13)
    for d in (4, 3, 5, 2, 6, 1, 7):
        zz = lax.rem(z + d, 8)
        post(D.at[lax.div(zz, 4), mod4(zz)], Z.at[d], z_s.at[d], z_r.at[d], zpeer[d])
    weights_near()
    conv(0)
    weights_z(14)
    weights_z(15)
    weights_wait()
    states_select()
    total = D[zh, zl].astype(F32)
    for d in (1, 7, 2, 6, 3, 5, 4):
        arrived(Z.at[d], z_r.at[d])
        total = total + Z[d].astype(F32)
    GA[c, zl] = total.astype(BF16)
    gather_z(GA, h_s, h_r)
    conv(1, 0, 3)
    gather_pair(GA, h_s, h_r)
    conv(1, 3, 4)
    conv(2, 0, 1)
    columns_select()
    conv(2, 1, 4)
    optimize()
    weights_sent()
    for copy in sends:
        copy.wait_send()


def exchange(latents, cotangent, gain, bias, weight, master, moment_one, moment_two, departing, partner):
    dma = pltpu.SemaphoreType.DMA
    vmem, smem = pl.BlockSpec(memory_space=pltpu.VMEM), pl.BlockSpec(memory_space=pltpu.SMEM)
    anywhere = pl.BlockSpec(memory_space=pl.ANY)
    half = pltpu.VMEM((PR, 640), BF16)
    state = jax.ShapeDtypeStruct((COLS, 2, ROWS), F32)
    return pl.pallas_call(
        exchange_kernel,
        out_shape=(jax.ShapeDtypeStruct((PIX, 640), BF16), state, state, state),
        in_specs=[vmem, anywhere, vmem, vmem, anywhere, vmem, vmem, vmem, smem, smem],
        out_specs=[vmem] * 4,
        scratch_shapes=[
            pltpu.VMEM((PIX + 64, 1920), BF16),
            pltpu.VMEM((1920, PIX), BF16),
            pltpu.VMEM((PIX + 64, 640), BF16),
            pltpu.VMEM((8 * ROWS, 640), BF16),
            pltpu.VMEM((8 * ROWS, 640), BF16),
            pltpu.VMEM((PIX, 640), F32),
            pltpu.VMEM((4, 4, 2, PR, 640), BF16),
            pltpu.VMEM((4, PR, 640), BF16),
            pltpu.VMEM((4, PR, 640), BF16),
            pltpu.VMEM((4, 2, PR, 640), BF16),
            pltpu.VMEM((4, 2, PR, 640), BF16),
            half,
            half,
            pltpu.VMEM((2, PR, 640), BF16),
            pltpu.VMEM((2, PR, 640), BF16),
            pltpu.VMEM((2, 4, GR, 640), BF16),
            pltpu.VMEM((8, GR, 640), BF16),
            pltpu.VMEM((3 * GR, ROWS), F32),
            pltpu.VMEM((2, 4, 3 * GR, ROWS), BF16),
            pltpu.VMEM((3, 3 * GR, ROWS), BF16),
            pltpu.VMEM((4, 3 * GR, ROWS), BF16),
            pltpu.VMEM((2, 4, GR, 640), BF16),
            pltpu.VMEM((4 * 48, 640), BF16),
            pltpu.VMEM((3, 48, 2 * PR), BF16),
            pltpu.VMEM((4, 48, 2 * PR), BF16),
            pltpu.VMEM((4, 2 * PR, ROWS), BF16),
            dma((32,)), dma((32,)),
            dma((7,)), dma((7,)),
            dma((7,)), dma((7,)),
            dma((18,)), dma((18,)),
            dma((20,)), dma((20,)),
            dma((10,)), dma((10,)),
            dma((20,)), dma((20,)),
            dma((2,)),
        ],
        compiler_params=pltpu.CompilerParams(
            collective_id=0, has_side_effects=True, vmem_limit_bytes=60 * 1024 * 1024
        ),
        name="exchange",
    )(latents, cotangent, gain, bias, weight, master, moment_one, moment_two, departing, partner)


def deliver_kernel(*refs):
    count = len(refs) // 2
    copies = [
        pltpu.make_async_copy(refs[n], refs[count + n], refs[-1].at[n]) for n in range(count)
    ]
    for copy in copies:
        copy.start()
    for copy in copies:
        copy.wait()


def deliver(*arrays):
    return pl.pallas_call(
        deliver_kernel,
        out_shape=tuple(jax.ShapeDtypeStruct(v.shape, v.dtype) for v in arrays),
        in_specs=[pl.BlockSpec(memory_space=pltpu.VMEM)] * len(arrays),
        out_specs=[pl.BlockSpec(memory_space=pl.ANY)] * len(arrays),
        scratch_shapes=[pltpu.SemaphoreType.DMA((len(arrays),))],
        name="deliver",
    )(*arrays)


def per_device(
    latents,
    cotangent,
    gn_gain,
    gn_bias,
    conv_weight,
    master,
    moment_one,
    moment_two,
    departing,
    partner,
):
    results = exchange(
        latents.reshape(PIX, -1),
        cotangent.reshape(PIX, -1),
        gn_gain,
        gn_bias,
        conv_weight,
        master,
        moment_one,
        moment_two,
        departing,
        partner,
    )
    forward, *states = deliver(*results)
    states = [jnp.transpose(state, (1, 0, 2))[None] for state in states]
    return (forward.reshape(cotangent.shape), *states)


def solution(mesh):
    return jax.shard_map(
        per_device,
        mesh=mesh,
        in_specs=(
            P(("rep", "shard"), None, None, None),
            P(("rep", "shard"), None, None, None),
            P(),
            P(),
            P("shard", None),
            P("rep", "shard"),
            P("rep", "shard"),
            P("rep", "shard"),
            P(),
            P(),
        ),
        out_specs=(
            P(("rep", "shard"), None, None, None),
            P("rep", None, None, "shard"),
            P("rep", None, None, "shard"),
            P("rep", None, None, "shard"),
        ),
        check_vma=False,
    )
```
